32 devices in a mesh: grp: 2 (over y), row: 4 (over z), head: 2 (over x), br: 2 (over core).
Axes of the slice: x: 2, y: 2, z: 4, core: 2. Of those that a mesh axis runs over, the one named last changes fastest.
Arguments:
- pair_acts: float32 [16, 8, 128], P(('grp', 'row', 'head')), parts along dimension 0, may hold values from -6 to 6
- alignment: float32 [64, 8, 256], P(('grp', 'br'), ('row', 'head')), parts along dimension 0, may hold values from -6 to 6
- align_mask: int32 [64, 8], P('grp', ('row', 'head')), parts along dimension 0, may hold values from 0 to 1
- residue_mask: int32 [16], P('grp'), parts along dimension 0, may hold values from 0 to 1, as said below
- align_gain: float32 [256], replicated, may hold values from 0.25 to 1.75
- outer_in: float32 [256, 64], replicated, may hold values from -0.375 to 0.375
- outer_out: float32 [1024, 128], replicated, may hold values from -1 to 1
- tri_gain: float32 [2, 128], replicated, may hold values from 0.25 to 1.75
- tri_in: float32 [2, 128, 4, 128], P(None, None, 'br'), may hold values from -5 to 5
- tri_bias: float32 [2, 128, 4], P(None, None, 'br'), may hold values from -0.5 to 0.5
- tri_out: float32 [2, 4, 32, 128], P(None, 'br'), may hold values from -0.5 to 0.5
- pair_cotangent: float32 [16, 8, 128], P(('grp', 'row', 'head')), parts along dimension 0, may hold values from -6 to 6
Outputs:
- pair_out: float32 [16, 8, 128], P(('grp', 'row', 'head')), parts along dimension 0
- pair_grad: float32 [16, 8, 128], P(('grp', 'row', 'head')), parts along dimension 0
The draws below stay inside these ranges and needn't reach their ends.
There are 2 independent parts, one for each index of `grp`. The reference program is written for one: setup_inputs(seed, part) draws one part's arguments, and reference() takes and returns one part's arrays. A program takes and returns all parts, laid end to end along the dimension named above; an argument that names none is the same for every part. Nothing has to cross between parts.
Inputs may be any that keep to these rules, and one draw needn't show every extreme that they name: `residue_mask`: 1 at residue 0, and 0 at one or more residues; `align_mask`: 1 at every residue of sequence 0 of each part.
All inputs are finite; a program needn't handle non-finite values.
Results may differ from the reference program's by a relative error of at most 0.0003.
Values sent between devices are 32-bit elements; how exact they have to be, the bound alone decides.
A program may use at most 64 MiB of HBM per device.

```python
import jax
import jax.numpy as jnp
from jax import lax

C = 128
CM = 256
OPC = 32
HEADS = 4
HD = 32
N = 8
S = 32


def draw_align_mask(key, part):
    draws_int = jax.random.randint(key, (S, N), 0, 4)
    leading = jnp.arange(S)[:, None] == 0
    return jnp.where(leading, 1, jnp.minimum(draws_int, 1)).astype(jnp.int32)


def draw_residue_mask(key, part):
    first_key = jax.random.fold_in(key, 11)
    second_key = jax.random.fold_in(key, 23)
    draws_int = jax.random.randint(first_key, (N,), 0, 4)
    dropped = jax.random.randint(second_key, (), 1, N)
    places = jnp.arange(N)
    values = jnp.minimum(draws_int, 1)
    values = jnp.where(places == 0, 1, values)
    values = jnp.where(places == dropped, 0, values)
    return values.astype(jnp.int32)


def draw_tri_in(key, part):
    weights = jax.random.truncated_normal(key, -4.0, 4.0, (2, C, HEADS, 4 * HD), jnp.float32) * C ** (-0.5)
    return weights


def shard_levels(own_key, dims, pieces, smallest, largest):
    def one(axis_at, shards_of):
        draws = jax.random.uniform(jax.random.fold_in(jax.random.fold_in(own_key, 6), axis_at), (shards_of,), jnp.float32, smallest / len(pieces), largest / len(pieces))
        return jnp.repeat(jnp.exp(draws), dims[axis_at] // shards_of).reshape((-1,) + (1,) * (len(dims) - axis_at - 1))

    gain = one(*pieces[0])
    for cut in pieces[1:]:
        gain = gain * one(*cut)
    return gain


def gaussian(own_key, dims, scale, most, split=(), dtype=jnp.bfloat16):
    entries = jax.random.normal(own_key, dims, jnp.float32) * scale
    if len(split) > 0:
        entries = shard_levels(own_key, dims, split, -0.22, 0.18) * entries
    return jnp.clip(entries, min=-most, max=most).astype(dtype)


def setup_inputs(seed: int = 0, part: int = 0) -> dict:
    keys = jax.random.split(jax.random.key(seed), 13)
    own_keys = jax.random.split(jax.random.fold_in(keys[12], part), 13)
    pair_acts = gaussian(own_keys[0], (N, N, C), 1.0, 6.0, ((0, 8),), jnp.float32)
    alignment = gaussian(own_keys[1], (S, N, CM), 1.0, 6.0, ((0, 2), (1, 8)), jnp.float32)
    align_mask = draw_align_mask(jax.random.fold_in(jax.random.fold_in(keys[12], part), 71), part)
    residue_mask = draw_residue_mask(jax.random.fold_in(jax.random.fold_in(keys[12], part), 71), part)
    align_gain = jnp.clip(1.0 + 0.15 * jax.random.normal(keys[4], (CM,), jnp.float32), 0.25, 1.75)
    outer_in = gaussian(keys[5], (CM, 2 * OPC), CM ** -0.5, 0.375, (), jnp.float32)
    outer_out = gaussian(keys[6], (OPC * OPC, C), OPC ** -0.5, 1.0, (), jnp.float32)
    tri_gain = jnp.clip(1.0 + 0.15 * jax.random.normal(keys[7], (2, C), jnp.float32), 0.25, 1.75)
    tri_in = draw_tri_in(jax.random.fold_in(keys[12], 71), part)
    tri_bias = gaussian(keys[9], (2, C, HEADS), C ** -0.5, 0.5, ((2, 2),), jnp.float32)
    tri_out = gaussian(keys[10], (2, HEADS, HD, C), (HEADS * HD) ** -0.5, 0.5, ((1, 2),), jnp.float32)
    pair_cotangent = gaussian(own_keys[11], (N, N, C), 1.0, 6.0, ((0, 8),), jnp.float32)
    return dict(pair_acts=pair_acts, alignment=alignment, align_mask=align_mask, residue_mask=residue_mask, align_gain=align_gain, outer_in=outer_in, outer_out=outer_out, tri_gain=tri_gain, tri_in=tri_in, tri_bias=tri_bias, tri_out=tri_out, pair_cotangent=pair_cotangent)


PRECISE = lax.Precision.HIGHEST
EPSILON = 1e-05
MASK_SHIFT = 1000000000.0

def normalize(values, scales):
    average = lax.optimization_barrier(jnp.mean(values, axis=-1, keepdims=True))
    centred = values - average
    spread = lax.optimization_barrier(jnp.mean(centred * centred, axis=-1, keepdims=True))
    return centred * lax.rsqrt(spread + EPSILON) * scales

def outer_update(alignment, align_mask, align_gain, outer_in, outer_out):
    mask_all = align_mask.astype(jnp.float32)
    normed = normalize(alignment, align_gain)
    projected = jnp.einsum('snc,ck->snk', normed, outer_in, precision=PRECISE)
    left_part = projected[..., :OPC] * mask_all[..., None]
    right_part = projected[..., OPC:] * mask_all[..., None]
    table = outer_out.reshape(OPC, OPC, C)
    mixed_left = jnp.einsum('sip,pqc->siqc', left_part, table, precision=PRECISE)
    summed = jnp.einsum('siqc,sjq->ijc', mixed_left, right_part, precision=PRECISE)
    counts = jnp.einsum('si,sj->ij', mask_all, mask_all, precision=PRECISE)
    return summed / counts[..., None]

def row_attention(rows_in, live, scales, weight_in, weight_bias, weight_out):
    normed = normalize(rows_in, scales)
    projected = jnp.einsum('ijc,chd->ijhd', normed, weight_in, precision=PRECISE)
    bias_full = jnp.einsum('jkc,ch->hjk', normed, weight_bias, precision=PRECISE)
    key_shift = (live - 1.0) * MASK_SHIFT
    scale_factor = HD ** (-0.5)

    def one_row(carried):
        row_proj, row_flag = carried
        queries = row_proj[:, :, :HD]
        key_proj = row_proj[:, :, HD:2 * HD]
        value_proj = row_proj[:, :, 2 * HD:3 * HD]
        gating = row_proj[:, :, 3 * HD:]
        logits = jnp.einsum('jhd,khd->hjk', queries, key_proj, precision=PRECISE) * scale_factor
        logits = logits + bias_full + key_shift
        attention = jax.nn.softmax(logits, axis=-1)
        attended = jnp.einsum('hjk,khd->jhd', attention, value_proj, precision=PRECISE)
        gated_out = jax.nn.sigmoid(gating) * attended
        update = jnp.einsum('jhd,hdc->jc', gated_out, weight_out, precision=PRECISE)
        return update * (row_flag * live)[:, None]
    updates = lax.map(one_row, (projected, live))
    return rows_in + updates

def reference(pair_acts, alignment, align_mask, residue_mask, align_gain, outer_in, outer_out, tri_gain, tri_in, tri_bias, tri_out, pair_cotangent):
    live = residue_mask.astype(jnp.float32)
    outer = outer_update(alignment, align_mask, align_gain, outer_in, outer_out)

    def forward(values):
        pair_one = values + outer
        pair_two = row_attention(pair_one, live, tri_gain[0], tri_in[0], tri_bias[0], tri_out[0])
        turned = row_attention(jnp.swapaxes(pair_two, 0, 1), live, tri_gain[1], tri_in[1], tri_bias[1], tri_out[1])
        return jnp.swapaxes(turned, 0, 1)
    pair_out, pull_back = jax.vjp(forward, pair_acts)
    pair_grad, = pull_back(pair_cotangent)
    return (pair_out, pair_grad)
```

```python
import functools

import jax
import jax.numpy as jnp
from jax import lax
from jax.experimental import pallas as pl
from jax.experimental.pallas import tpu as pltpu
from jax.sharding import PartitionSpec as P

OPC = 32


PRECISE = lax.Precision.HIGHEST
EPSILON = 1e-05
MASK_SHIFT = 1000000000.0


def normalize(values, scales):
    average = jnp.mean(values, axis=-1, keepdims=True)
    centred = values - average
    spread = jnp.mean(centred * centred, axis=-1, keepdims=True)
    return centred * lax.rsqrt(spread + EPSILON) * scales


def core_total(values):
    return lax.psum(values, "br")


def reorient(values):
    turned = jnp.swapaxes(values, 0, 1)
    return lax.all_to_all(turned, ("row", "head"), split_axis=0, concat_axis=1, tiled=True)


def prepare(values, scales, weight_in, weight_bias):
    normed = normalize(values, scales)
    projected = jnp.einsum("ijc,chd->ijhd", normed, weight_in, precision=PRECISE)
    bias_local = jnp.einsum("jkc,ch->hjk", normed, weight_bias, precision=PRECISE)
    return (projected, bias_local)


def attend(projected, bias_full, key_shift, weight_out):
    head_size = projected.shape[-1] // 4
    queries = projected[..., :head_size]
    key_proj = projected[..., head_size : 2 * head_size]
    value_proj = projected[..., 2 * head_size : 3 * head_size]
    gating = projected[..., 3 * head_size :]
    logits = jnp.einsum("ijhd,ikhd->ihjk", queries, key_proj, precision=PRECISE) * head_size ** (
        -0.5
    )
    logits = logits + bias_full[None] + key_shift
    attention = jax.nn.softmax(logits, axis=-1)
    attended = jnp.einsum("ihjk,ikhd->ijhd", attention, value_proj, precision=PRECISE)
    gated_out = jax.nn.sigmoid(gating) * attended
    return jnp.einsum("ijhd,hdc->ijc", gated_out, weight_out, precision=PRECISE)


def tri_forward(rows_in, scales, weight_in, weight_bias, weight_out, key_shift, pair_mask):

    def local_prep(values):
        return prepare(values, scales, weight_in, weight_bias)

    (projected, bias_local), pull_prep = jax.vjp(local_prep, rows_in)
    bias_full = lax.all_gather(bias_local, ("row", "head"), axis=1, tiled=True)

    def local_attend(proj_in, bias_in):
        return attend(proj_in, bias_in, key_shift, weight_out)

    partial_out, pull_attend = jax.vjp(local_attend, projected, bias_full)
    total_out = core_total(partial_out)
    return (rows_in + total_out * pair_mask, (pull_prep, pull_attend))


def tri_backward(grad_out, saved, pair_mask):
    pull_prep, pull_attend = saved
    grad_proj, grad_bias = pull_attend(grad_out * pair_mask)
    grad_local = lax.psum_scatter(grad_bias, ("row", "head"), scatter_dimension=1, tiled=True)
    (grad_rows,) = pull_prep((grad_proj, grad_local))
    return grad_out + core_total(grad_rows)


def spread_body(
    pair_acts,
    alignment,
    align_mask,
    residue_mask,
    align_gain,
    outer_in,
    outer_out,
    tri_gain,
    tri_in,
    tri_bias,
    tri_out,
    pair_cotangent,
):
    row_count = pair_acts.shape[0]
    live = residue_mask.astype(jnp.float32)
    key_shift = (live - 1.0) * MASK_SHIFT
    row_live = lax.dynamic_slice_in_dim(
        live, lax.axis_index(("row", "head")) * row_count, row_count, 0
    )
    pair_mask = row_live[:, None, None] * live[None, :, None]
    seq_count = alignment.shape[0]
    mask_all = align_mask.astype(jnp.float32)
    mask_own = lax.dynamic_slice_in_dim(mask_all, lax.axis_index("br") * seq_count, seq_count, 0)
    normed = normalize(alignment, align_gain)
    projected = jnp.einsum("snc,ck->snk", normed, outer_in, precision=PRECISE)
    left_part = projected[..., :OPC] * mask_own[..., None]
    right_part = jnp.swapaxes(projected[..., OPC:] * mask_own[..., None], 1, 2)
    right_all, mask_cols = (
        lax.all_gather(right_part, ("row", "head"), axis=2, tiled=True),
        lax.all_gather(mask_all, ("row", "head"), axis=1, tiled=True),
    )
    counts = jnp.einsum("si,sj->ij", mask_all, mask_cols, precision=PRECISE)
    table = outer_out.reshape(OPC, OPC, outer_out.shape[-1])
    mixed_left = jnp.einsum("sip,pqc->siqc", left_part, table, precision=PRECISE)
    partial_outer = jnp.einsum("siqc,sqj->ijc", mixed_left, right_all, precision=PRECISE)
    outer_sum = core_total(partial_outer)
    pair_one = pair_acts + outer_sum / counts[..., None]
    pair_two, saved_start = tri_forward(
        pair_one, tri_gain[0], tri_in[0], tri_bias[0], tri_out[0], key_shift, pair_mask
    )
    turned_two = reorient(pair_two)
    turned_three, saved_end = tri_forward(
        turned_two, tri_gain[1], tri_in[1], tri_bias[1], tri_out[1], key_shift, pair_mask
    )
    pair_out = reorient(turned_three)
    grad_turned = reorient(pair_cotangent)
    grad_turned = tri_backward(grad_turned, saved_end, pair_mask)
    grad_two = reorient(grad_turned)
    pair_grad = tri_backward(grad_two, saved_start, pair_mask)
    return (pair_out, pair_grad)


MESH_ID = pl.DeviceIdType.MESH
FUSED_BYTES = 1 << 20
NN = ((1,), (0,))
NT = ((1,), (1,))
TN = ((0,), (0,))


def split(values):
    high = values.astype(jnp.bfloat16)
    low = (values - high.astype(jnp.float32)).astype(jnp.bfloat16)
    return (high, low)


def pair_dot(first, second, dims):
    def one(a, b):
        return lax.dot_general(a, b, (dims, ((), ())), preferred_element_type=jnp.float32)

    a = jnp.concatenate([first[0], first[1], first[0]], axis=dims[0][0])
    b = jnp.concatenate([second[0], second[0], second[1]], axis=dims[1][0])
    return one(a, b)


def standardize(values):
    average = jnp.mean(values, axis=-1, keepdims=True)
    centred = values - average
    spread = jnp.mean(centred * centred, axis=-1, keepdims=True)
    inverse = lax.rsqrt(spread + EPSILON)
    return (centred * inverse, inverse)


def fused_kernel(
    sizes,
    live_hbm,
    acts_hbm,
    align_hbm,
    mask_hbm,
    gain_hbm,
    outer_in_hbm,
    outer_out_hbm,
    tri_gain_hbm,
    tri_in_hbm,
    tri_bias_hbm,
    tri_out_hbm,
    cot_hbm,
    out_ref,
    live_ref,
    pair_all,
    proj_all,
    align_v,
    mask_v,
    gain_v,
    outer_in_v,
    outer_out_v,
    tri_gain_v,
    tri_in_all,
    tri_bias_all,
    tri_out_all,
    table_hi,
    table_lo,
    wide_hi,
    wide_lo,
    turn_v,
    mixed_v,
    load_sems,
    send_sems,
    recv_sems,
):
    rows_n, heads_n, cores_n = sizes
    count = rows_n * heads_n
    chan = pair_all.shape[-1]
    my_row = lax.axis_index("row")
    my_head = lax.axis_index("head")
    my_core = lax.axis_index("br")
    me = my_row * heads_n + my_head
    seqs = align_v.shape[0]
    half = tri_in_all.shape[3]
    head_count = half * cores_n
    size = tri_in_all.shape[4] // 4
    width = head_count * size

    own_pair = pair_all.at[my_core, me, 0:count]
    loads = [
        pltpu.make_async_copy(align_hbm, align_v, load_sems.at[0]),
        pltpu.make_async_copy(gain_hbm, gain_v, load_sems.at[1]),
        pltpu.make_async_copy(outer_in_hbm, outer_in_v, load_sems.at[2]),
        pltpu.make_async_copy(mask_hbm, mask_v, load_sems.at[3]),
        pltpu.make_async_copy(acts_hbm.at[0], own_pair, load_sems.at[4]),
        pltpu.make_async_copy(tri_in_hbm, tri_in_all.at[my_core], load_sems.at[5]),
        pltpu.make_async_copy(tri_bias_hbm, tri_bias_all.at[my_core], load_sems.at[6]),
        pltpu.make_async_copy(tri_out_hbm, tri_out_all.at[my_core], load_sems.at[7]),
        pltpu.make_async_copy(live_hbm, live_ref, load_sems.at[8]),
        pltpu.make_async_copy(outer_out_hbm, outer_out_v, load_sems.at[9]),
        pltpu.make_async_copy(tri_gain_hbm, tri_gain_v, load_sems.at[10]),
    ]
    for load in loads[:4]:
        load.start()

    @pl.when(my_core == 0)
    def _():
        loads[4].start()

    @pl.when(my_core != 0)
    def _():
        pltpu.make_async_copy(cot_hbm.at[0], own_pair, load_sems.at[4]).start()

    peers = [
        (dr, dh, db)
        for dr in range(rows_n)
        for dh in range(heads_n)
        for db in range(cores_n)
        if (dr, dh, db) != (0, 0, 0)
    ]

    def place(offset):
        dr, dh, db = offset
        return (
            lax.rem(my_row + dr, rows_n),
            lax.rem(my_head + dh, heads_n),
            lax.rem(my_core + db, cores_n),
        )

    def target(offset):
        row, head, core = place(offset)
        return {"row": row, "head": head, "br": core}

    ordered = sorted(peers, key=lambda o: -(min(o[0], rows_n - o[0]) + o[1]))
    barrier = pltpu.get_barrier_semaphore()
    for offset in ordered:
        pl.semaphore_signal(barrier, inc=1, device_id=target(offset), device_id_type=MESH_ID)
    for load in loads[5:]:
        load.start()

    def remote(src, dst, which, offset):
        return pltpu.make_async_remote_copy(
            src_ref=src,
            dst_ref=dst,
            send_sem=send_sems.at[which],
            recv_sem=recv_sems.at[which],
            device_id=target(offset),
            device_id_type=MESH_ID,
        )

    aside = (0, 0, 1)
    other_core = lax.rem(my_core + 1, cores_n)
    near = [offset for offset in ordered if offset[2] == 0]
    for load in loads[:5]:
        load.wait()
    pl.semaphore_wait(barrier, len(peers))

    mask_f = mask_v[...].astype(jnp.float32)
    depth = mask_f.shape[1]
    pair_all[my_core, me, count : count + 1] = jnp.concatenate(
        [mask_f, jnp.zeros((1, chan - depth), jnp.float32)], axis=1
    )
    mine = pair_all.at[my_core, me, 0 : count + 1]
    for offset in near:
        remote(mine, mine, 0, offset).start()
    weight_copies = [
        remote(src, dst.at[my_core], 3 + which, aside)
        for which, (src, dst) in enumerate(
            ((tri_in_hbm, tri_in_all), (tri_bias_hbm, tri_bias_all), (tri_out_hbm, tri_out_all))
        )
    ]
    for copy in weight_copies:
        copy.start()

    pieces = seqs // 8
    aligned = align_v[:, 0, :]
    centred = aligned - jnp.mean(aligned, axis=-1, keepdims=True)
    inverse = lax.rsqrt(jnp.mean(centred * centred, axis=-1, keepdims=True) + EPSILON)
    lane = lax.broadcasted_iota(jnp.int32, (seqs, depth), 1)
    own_s = lax.broadcasted_iota(jnp.int32, (seqs, depth), 0) + my_core * seqs
    mask_own = jnp.sum(jnp.where(lane == own_s, mask_f, 0.0), axis=1, keepdims=True)
    in_hi, in_lo = split(outer_in_v[...] * gain_v[...])
    in_hi = jnp.concatenate([in_hi] * pieces, axis=0)
    in_lo = jnp.concatenate([in_lo] * pieces, axis=0)
    rows_hi, rows_lo = split(centred)

    def against(a, b):
        return lax.dot_general(a, b, (NT, ((), ())), preferred_element_type=jnp.float32)

    both = against(jnp.concatenate([rows_hi, rows_lo], axis=0), in_hi)
    projected = both[:seqs] + both[seqs:] + against(rows_hi, in_lo)
    projected = projected * (inverse * mask_own)
    piece_at = lax.broadcasted_iota(jnp.int32, (8, chan), 1) // (2 * OPC)
    packed = projected[0:8]
    for piece in range(1, pieces):
        packed = jnp.where(piece_at == piece, projected[8 * piece : 8 * piece + 8], packed)
    slot = my_core * count + me
    proj_all[slot] = packed
    for offset in ordered:
        remote(proj_all.at[slot], proj_all.at[slot], 1, offset).start()
    for load in loads[5:]:
        load.wait()

    for q in range(OPC):
        high, low = split(outer_out_v[pl.ds(q, OPC, stride=OPC), :])
        table_hi[q * OPC : (q + 1) * OPC] = high
        table_lo[q * OPC : (q + 1) * OPC] = low

    pairs = count * count
    lanes = head_count * pairs
    tile_row = lax.broadcasted_iota(jnp.int32, (count, count, lanes), 0)
    lane_at = lax.rem(lax.broadcasted_iota(jnp.int32, (count, count, lanes), 2), pairs)
    at_first = tile_row == lane_at // count
    at_second = tile_row == lax.rem(lane_at, count)
    live = [live_ref[n].astype(jnp.float32) for n in range(count)]
    key_at = lax.broadcasted_iota(jnp.int32, (count, lanes), 0)
    first_at = lax.broadcasted_iota(jnp.int32, (count, count, chan), 0)
    second_at = lax.broadcasted_iota(jnp.int32, (count, count, chan), 1)
    key_live = jnp.zeros((count, lanes), jnp.float32)
    live_first = jnp.zeros((count, count, chan), jnp.float32)
    live_second = jnp.zeros((count, count, chan), jnp.float32)
    for n in range(count):
        key_live = jnp.where(key_at == n, live[n], key_live)
        live_first = jnp.where(first_at == n, live[n], live_first)
        live_second = jnp.where(second_at == n, live[n], live_second)
    key_shift = (key_live - 1.0) * MASK_SHIFT
    pair_mask = (live_first * live_second).reshape(pairs, chan)
    lane_head = lax.broadcasted_iota(jnp.int32, (pairs, width), 1) // size

    def heads_apart(values):
        return jnp.concatenate(
            [jnp.where(lane_head == h, values, 0.0) for h in range(head_count)], axis=0
        )

    def heads_together(values):
        total = jnp.where(lane_head == 0, values[0:pairs], 0.0)
        for h in range(1, head_count):
            total = jnp.where(lane_head == h, values[h * pairs : (h + 1) * pairs], total)
        return total

    def spread_over(values, where):
        return jnp.where(where, values[None], 0.0).reshape(pairs, lanes)

    def fold(values, where):
        return jnp.sum(jnp.where(where, values.reshape(count, count, lanes), 0.0), axis=0)

    for copy in weight_copies:
        copy.wait_recv()

    outs = []
    for t in range(2):
        blocks = []
        for h in range(head_count):
            blocks.append(tri_in_all[h // half, t, :, h % half, :])
        for block in range(4):
            columns = jnp.concatenate(
                [b[:, block * size : (block + 1) * size] for b in blocks], axis=1
            )
            high, low = split(columns)
            wide_hi[t, :, block * width : (block + 1) * width] = high
            wide_lo[t, :, block * width : (block + 1) * width] = low
        bias_rows = jnp.concatenate(
            [tri_bias_all[core, t] for core in range(cores_n)]
            + [jnp.zeros((chan - head_count, chan), jnp.float32)],
            axis=0,
        )
        bias_turned = bias_rows.T
        bias_columns = jnp.concatenate(
            [
                jnp.broadcast_to(bias_turned[:, h : h + 1], (chan, pairs))
                for h in range(head_count)
            ],
            axis=1,
        )
        high, low = split(bias_columns)
        wide_hi[t, :, 4 * width :] = high
        wide_lo[t, :, 4 * width :] = low
        outs.append(
            split(
                jnp.concatenate(
                    [tri_out_all[h // half, t, h % half] for h in range(head_count)], axis=0
                )
            )
        )

    gathered = pair_all.at[my_core, 0 : count - 1, 0 : count + 1]
    pair_total = remote(gathered, gathered, 0, aside)
    pair_total.wait_recv()
    forward_copy = remote(
        pair_all.at[my_core, :, 0 : count + 1], pair_all.at[my_core, :, 0 : count + 1], 2, aside
    )
    forward_copy.start()
    shared = proj_all.at[0 : cores_n * count - 1]
    proj_total = remote(shared, shared, 1, aside)
    proj_total.wait_recv()

    left_tiles = []
    right_tiles = []
    for core in range(cores_n):
        for piece in range(pieces):
            base = piece * 2 * OPC
            left_tiles.append(
                jnp.concatenate(
                    [proj_all[core * count + n, :, base : base + OPC] for n in range(count)], axis=1
                )
            )
            right_tiles.append(
                jnp.concatenate(
                    [
                        proj_all[core * count + n, :, base + OPC : base + 2 * OPC]
                        for n in range(count)
                    ],
                    axis=1,
                )
            )
    left = jnp.concatenate(left_tiles, axis=0)
    right = jnp.concatenate(right_tiles, axis=0)
    mixed = pair_dot(split(right), split(left), TN)
    for block in range(mixed_v.shape[0]):
        mixed_v[block] = mixed[:, block * chan : (block + 1) * chan]
    strips = [[] for _ in range(count)]
    for q in range(OPC):
        for block in range(mixed_v.shape[0]):
            tile = mixed_v[block, pl.ds(q, count, stride=OPC), :]
            for n in range(chan // OPC):
                strips[block * (chan // OPC) + n].append(tile[:, n * OPC : (n + 1) * OPC])
    crossed = jnp.concatenate([jnp.concatenate(s, axis=1) for s in strips], axis=0)
    summed = pair_dot(split(crossed), (table_hi[...], table_lo[...]), NN)
    mask_rows = jnp.concatenate(
        [pair_all[my_core, n, count : count + 1] for n in range(count)], axis=0
    )
    counts = jnp.sum(mask_rows[:, None, :] * mask_rows[None, :, :], axis=-1, keepdims=True)
    forward_copy.wait_recv()
    acts = jnp.concatenate([pair_all[0, n, 0:count] for n in range(count)], axis=0)
    pair_one = acts + summed / counts.reshape(pairs, 1)

    def turn(values):
        turn_v[...] = values
        return jnp.concatenate(
            [turn_v[pl.ds(n, count, stride=count), :] for n in range(count)], axis=0
        )

    scale = size ** (-0.5)

    def forward(x, t):
        gain = tri_gain_v[t : t + 1]
        hat, inverse = standardize(x)
        weights = (wide_hi[t], wide_lo[t])
        projected = pair_dot(split(hat * gain), weights, NN)
        query = projected[:, 0:width] * scale
        key = split(projected[:, width : 2 * width])
        value = split(projected[:, 2 * width : 3 * width])
        gate = jax.nn.sigmoid(projected[:, 3 * width : 4 * width])
        bias = fold(projected[:, 4 * width :], at_second)
        query_apart = split(heads_apart(query))
        logits = fold(pair_dot(key, query_apart, NT), at_first) + bias + key_shift
        top = jnp.max(logits, axis=0, keepdims=True)
        exps = jnp.exp(logits - top)
        probs = exps / jnp.sum(exps, axis=0, keepdims=True)
        probs_wide = split(spread_over(probs, at_first))
        attended = heads_together(pair_dot(probs_wide, value, TN))
        update = pair_dot(split(gate * attended), outs[t], NN)
        saved = (hat, inverse, gain, weights, key, value, gate, query_apart, probs, probs_wide, attended)
        return (x + update * pair_mask, saved)

    def gated_of(grad, t):
        return pair_dot(split(grad * pair_mask), outs[t], NT)

    def backward(grad, d_gated, t, saved):
        hat, inverse, gain, weights, key, value, gate, query_apart, probs, probs_wide, attended = saved
        d_gate = d_gated * attended * gate * (1.0 - gate)
        d_apart = split(heads_apart(d_gated * gate))
        d_probs = fold(pair_dot(value, d_apart, NT), at_first)
        d_value = pair_dot(probs_wide, d_apart, NN)
        d_logits = probs * (d_probs - jnp.sum(probs * d_probs, axis=0, keepdims=True))
        d_wide = split(spread_over(d_logits, at_first))
        d_key = pair_dot(d_wide, query_apart, NN)
        d_query = heads_together(pair_dot(d_wide, key, TN)) * scale
        d_bias = spread_over(d_logits, at_second)

        def through(values, start, stop):
            return pair_dot(split(values), (weights[0][:, start:stop], weights[1][:, start:stop]), NT)

        early = through(jnp.concatenate([d_value, d_gate], axis=1), 2 * width, 4 * width)
        middle = through(d_bias, 4 * width, 4 * width + lanes)
        late = through(jnp.concatenate([d_query, d_key], axis=1), 0, 2 * width)
        d_normed = (early + middle + late) * gain
        mean_d = jnp.mean(d_normed, axis=-1, keepdims=True)
        mean_dh = jnp.mean(d_normed * hat, axis=-1, keepdims=True)
        return grad + inverse * (d_normed - mean_d - hat * mean_dh)

    pair_two, saved_start = forward(pair_one, 0)
    cot = jnp.concatenate([pair_all[1, :, n, :] for n in range(count)], axis=0)
    cot_gated = gated_of(cot, 1)
    turned, saved_end = forward(turn(pair_two), 1)
    turn_v[...] = turned
    out_ref[0] = turn_v[pl.ds(me, count, stride=count), :]

    grad_two = turn(backward(cot, cot_gated, 1, saved_end))
    turn_v[...] = backward(grad_two, gated_of(grad_two, 0), 0, saved_start)
    out_ref[1] = turn_v[pl.ds(pl.multiple_of(me * count, count), count), :]

    for copy in (pair_total, proj_total, forward_copy, *weight_copies):
        copy.wait_send()


def fused_body(shape, args):
    (
        pair_acts,
        alignment,
        align_mask,
        residue_mask,
        align_gain,
        outer_in,
        outer_out,
        tri_gain,
        tri_in,
        tri_bias,
        tri_out,
        pair_cotangent,
    ) = args
    rows_n, heads_n, cores_n = shape["row"], shape["head"], shape["br"]
    count = rows_n * heads_n
    chan = pair_acts.shape[-1]
    seqs = alignment.shape[0]
    half, size = tri_in.shape[2], tri_in.shape[3] // 4
    head_count = half * cores_n
    lanes = head_count * count * count
    wide = 4 * head_count * size + lanes
    f32, b16 = jnp.float32, jnp.bfloat16
    anywhere = pl.BlockSpec(memory_space=pl.ANY)
    here = pl.BlockSpec(memory_space=pltpu.VMEM)
    dma = pltpu.SemaphoreType.DMA
    scratch = [
        pltpu.SMEM(residue_mask.shape, jnp.int32),
        pltpu.VMEM((cores_n, count, count + 8, chan), f32),
        pltpu.VMEM((cores_n * count, 8, chan), f32),
        pltpu.VMEM(alignment.shape, f32),
        pltpu.VMEM(align_mask.shape[::-1], jnp.int32),
        pltpu.VMEM((1, align_gain.shape[0]), f32),
        pltpu.VMEM(outer_in.shape[::-1], f32),
        pltpu.VMEM(outer_out.shape, f32),
        pltpu.VMEM(tri_gain.shape, f32),
        pltpu.VMEM((cores_n,) + tri_in.shape, f32),
        pltpu.VMEM((cores_n, 2, half, chan), f32),
        pltpu.VMEM((cores_n,) + tri_out.shape, f32),
        pltpu.VMEM(outer_out.shape, b16),
        pltpu.VMEM(outer_out.shape, b16),
        pltpu.VMEM((2, chan, wide), b16),
        pltpu.VMEM((2, chan, wide), b16),
        pltpu.VMEM((count * count, chan), f32),
        pltpu.VMEM((count * OPC // chan, count * OPC, chan), f32),
        dma((11,)),
        dma((6,)),
        dma((6,)),
    ]
    both = pl.pallas_call(
        functools.partial(fused_kernel, (rows_n, heads_n, cores_n)),
        out_shape=pltpu.VMEM((2,) + pair_acts.shape[1:], f32),
        in_specs=[anywhere] * 12,
        out_specs=here,
        scratch_shapes=scratch,
        compiler_params=pltpu.CompilerParams(collective_id=0, has_side_effects=True),
    )(
        residue_mask,
        pair_acts,
        alignment,
        align_mask.T,
        align_gain[None],
        outer_in.T,
        outer_out,
        tri_gain,
        tri_in,
        jnp.swapaxes(tri_bias, 1, 2),
        tri_out,
        pair_cotangent,
    )
    return (both[0:1], both[1:2])


def dispatch(shape, *args):
    pair_acts, alignment, align_mask, tri_in = args[0], args[1], args[2], args[8]
    count = pair_acts.shape[1]
    head_count = tri_in.shape[2] * shape["br"]
    chan = pair_acts.shape[-1]
    fits = (
        pair_acts.shape[0] == 1
        and shape["br"] == 2
        and alignment.shape[1] == 1
        and count % 8 == 0
        and alignment.shape[0] // 8 * 2 * OPC == chan
        and align_mask.shape[0] <= chan
        and head_count * (tri_in.shape[3] // 4) == chan
        and head_count * count**4 * 4 <= FUSED_BYTES
    )
    return fused_body(shape, args) if fits else spread_body(*args)


def solution(mesh):
    in_specs = (
        P(("grp", "row", "head"), None, None),
        P(("grp", "br"), ("row", "head"), None),
        P("grp", ("row", "head")),
        P("grp"),
        P(),
        P(),
        P(),
        P(),
        P(None, None, "br", None),
        P(None, None, "br"),
        P(None, "br", None, None),
        P(("grp", "row", "head"), None, None),
    )
    out_specs = (P(("grp", "row", "head"), None, None), P(("grp", "row", "head"), None, None))
    return jax.shard_map(functools.partial(dispatch, dict(mesh.shape)), mesh=mesh, in_specs=in_specs, out_specs=out_specs, check_vma=False)
```

```python
import functools

import jax
import jax.numpy as jnp
from jax import lax
from jax.experimental import pallas as pl
from jax.experimental.pallas import tpu as pltpu
from jax.sharding import PartitionSpec as P

OPC = 32


PRECISE = lax.Precision.HIGHEST
EPSILON = 1e-05
MASK_SHIFT = 1000000000.0


def normalize(values, scales):
    average = jnp.mean(values, axis=-1, keepdims=True)
    centred = values - average
    spread = jnp.mean(centred * centred, axis=-1, keepdims=True)
    return centred * lax.rsqrt(spread + EPSILON) * scales


def core_total(values):
    return lax.psum(values, "br")


def reorient(values):
    turned = jnp.swapaxes(values, 0, 1)
    return lax.all_to_all(turned, ("row", "head"), split_axis=0, concat_axis=1, tiled=True)


def prepare(values, scales, weight_in, weight_bias):
    normed = normalize(values, scales)
    projected = jnp.einsum("ijc,chd->ijhd", normed, weight_in, precision=PRECISE)
    bias_local = jnp.einsum("jkc,ch->hjk", normed, weight_bias, precision=PRECISE)
    return (projected, bias_local)


def attend(projected, bias_full, key_shift, weight_out):
    head_size = projected.shape[-1] // 4
    queries = projected[..., :head_size]
    key_proj = projected[..., head_size : 2 * head_size]
    value_proj = projected[..., 2 * head_size : 3 * head_size]
    gating = projected[..., 3 * head_size :]
    logits = jnp.einsum("ijhd,ikhd->ihjk", queries, key_proj, precision=PRECISE) * head_size ** (
        -0.5
    )
    logits = logits + bias_full[None] + key_shift
    attention = jax.nn.softmax(logits, axis=-1)
    attended = jnp.einsum("ihjk,ikhd->ijhd", attention, value_proj, precision=PRECISE)
    gated_out = jax.nn.sigmoid(gating) * attended
    return jnp.einsum("ijhd,hdc->ijc", gated_out, weight_out, precision=PRECISE)


def tri_forward(rows_in, scales, weight_in, weight_bias, weight_out, key_shift, pair_mask):

    def local_prep(values):
        return prepare(values, scales, weight_in, weight_bias)

    (projected, bias_local), pull_prep = jax.vjp(local_prep, rows_in)
    bias_full = lax.all_gather(bias_local, ("row", "head"), axis=1, tiled=True)

    def local_attend(proj_in, bias_in):
        return attend(proj_in, bias_in, key_shift, weight_out)

    partial_out, pull_attend = jax.vjp(local_attend, projected, bias_full)
    total_out = core_total(partial_out)
    return (rows_in + total_out * pair_mask, (pull_prep, pull_attend))


def tri_backward(grad_out, saved, pair_mask):
    pull_prep, pull_attend = saved
    grad_proj, grad_bias = pull_attend(grad_out * pair_mask)
    grad_local = lax.psum_scatter(grad_bias, ("row", "head"), scatter_dimension=1, tiled=True)
    (grad_rows,) = pull_prep((grad_proj, grad_local))
    return grad_out + core_total(grad_rows)


def spread_body(
    pair_acts,
    alignment,
    align_mask,
    residue_mask,
    align_gain,
    outer_in,
    outer_out,
    tri_gain,
    tri_in,
    tri_bias,
    tri_out,
    pair_cotangent,
):
    row_count = pair_acts.shape[0]
    live = residue_mask.astype(jnp.float32)
    key_shift = (live - 1.0) * MASK_SHIFT
    row_live = lax.dynamic_slice_in_dim(
        live, lax.axis_index(("row", "head")) * row_count, row_count, 0
    )
    pair_mask = row_live[:, None, None] * live[None, :, None]
    seq_count = alignment.shape[0]
    mask_all = align_mask.astype(jnp.float32)
    mask_own = lax.dynamic_slice_in_dim(mask_all, lax.axis_index("br") * seq_count, seq_count, 0)
    normed = normalize(alignment, align_gain)
    projected = jnp.einsum("snc,ck->snk", normed, outer_in, precision=PRECISE)
    left_part = projected[..., :OPC] * mask_own[..., None]
    right_part = jnp.swapaxes(projected[..., OPC:] * mask_own[..., None], 1, 2)
    right_all, mask_cols = (
        lax.all_gather(right_part, ("row", "head"), axis=2, tiled=True),
        lax.all_gather(mask_all, ("row", "head"), axis=1, tiled=True),
    )
    counts = jnp.einsum("si,sj->ij", mask_all, mask_cols, precision=PRECISE)
    table = outer_out.reshape(OPC, OPC, outer_out.shape[-1])
    mixed_left = jnp.einsum("sip,pqc->siqc", left_part, table, precision=PRECISE)
    partial_outer = jnp.einsum("siqc,sqj->ijc", mixed_left, right_all, precision=PRECISE)
    outer_sum = core_total(partial_outer)
    pair_one = pair_acts + outer_sum / counts[..., None]
    pair_two, saved_start = tri_forward(
        pair_one, tri_gain[0], tri_in[0], tri_bias[0], tri_out[0], key_shift, pair_mask
    )
    turned_two = reorient(pair_two)
    turned_three, saved_end = tri_forward(
        turned_two, tri_gain[1], tri_in[1], tri_bias[1], tri_out[1], key_shift, pair_mask
    )
    pair_out = reorient(turned_three)
    grad_turned = reorient(pair_cotangent)
    grad_turned = tri_backward(grad_turned, saved_end, pair_mask)
    grad_two = reorient(grad_turned)
    pair_grad = tri_backward(grad_two, saved_start, pair_mask)
    return (pair_out, pair_grad)


MESH_ID = pl.DeviceIdType.MESH
FUSED_BYTES = 1 << 20
NN = ((1,), (0,))
NT = ((1,), (1,))
TN = ((0,), (0,))


def split(values):
    high = values.astype(jnp.bfloat16)
    low = (values - high.astype(jnp.float32)).astype(jnp.bfloat16)
    return (high, low)


def pair_dot(first, second, dims):
    def one(a, b):
        return lax.dot_general(a, b, (dims, ((), ())), preferred_element_type=jnp.float32)

    a = jnp.concatenate([first[0], first[1], first[0]], axis=dims[0][0])
    b = jnp.concatenate([second[0], second[0], second[1]], axis=dims[1][0])
    return one(a, b)


def plain_dot(a, b, dims):
    return lax.dot_general(a, b, (dims, ((), ())), preferred_element_type=jnp.float32)


def doubled(values):
    high, low = split(values)
    return jnp.concatenate(
        [
            jnp.concatenate([high, high], axis=1),
            jnp.concatenate([low, jnp.zeros_like(low)], axis=1),
        ],
        axis=0,
    )


def stacked(values, axis):
    return jnp.concatenate(split(values), axis=axis)


def halves(values):
    rows = values.shape[0] // 2
    return values[:rows] + values[rows:]


def quarters(values):
    rows, columns = values.shape[0] // 2, values.shape[1] // 2
    return values[:rows, :columns] + values[rows:, :columns] + values[:rows, columns:]


def fused_kernel(
    sizes,
    live_hbm,
    acts_hbm,
    align_hbm,
    mask_hbm,
    gain_hbm,
    outer_in_hbm,
    outer_out_hbm,
    tri_gain_hbm,
    tri_in_hbm,
    tri_bias_hbm,
    tri_out_hbm,
    cot_hbm,
    out_ref,
    live_ref,
    pair_all,
    proj_all,
    align_v,
    mask_v,
    gain_v,
    outer_in_v,
    outer_out_v,
    tri_gain_v,
    tri_in_all,
    tri_bias_all,
    tri_out_all,
    table_v,
    wide_v,
    cross_v,
    out_v,
    back_v,
    turn_v,
    mixed_v,
    load_sems,
    send_sems,
    recv_sems,
):
    rows_n, heads_n, cores_n = sizes
    count = rows_n * heads_n
    chan = pair_all.shape[-1]
    my_row = lax.axis_index("row")
    my_head = lax.axis_index("head")
    my_core = lax.axis_index("br")
    me = my_row * heads_n + my_head
    seqs = align_v.shape[0]
    half = tri_in_all.shape[3]
    head_count = half * cores_n
    size = tri_in_all.shape[4] // 4
    width = head_count * size

    own_pair = pair_all.at[my_core, me, 0:count]
    loads = [
        pltpu.make_async_copy(align_hbm, align_v, load_sems.at[0]),
        pltpu.make_async_copy(gain_hbm, gain_v, load_sems.at[1]),
        pltpu.make_async_copy(outer_in_hbm, outer_in_v, load_sems.at[2]),
        pltpu.make_async_copy(mask_hbm, mask_v, load_sems.at[3]),
        pltpu.make_async_copy(acts_hbm.at[0], own_pair, load_sems.at[4]),
        pltpu.make_async_copy(tri_in_hbm, tri_in_all.at[my_core], load_sems.at[5]),
        pltpu.make_async_copy(tri_bias_hbm, tri_bias_all.at[my_core], load_sems.at[6]),
        pltpu.make_async_copy(tri_out_hbm, tri_out_all.at[my_core], load_sems.at[7]),
        pltpu.make_async_copy(live_hbm, live_ref, load_sems.at[8]),
        pltpu.make_async_copy(outer_out_hbm, outer_out_v, load_sems.at[9]),
        pltpu.make_async_copy(tri_gain_hbm, tri_gain_v, load_sems.at[10]),
    ]
    for load in loads[:4]:
        load.start()

    @pl.when(my_core == 0)
    def _():
        loads[4].start()

    @pl.when(my_core != 0)
    def _():
        pltpu.make_async_copy(cot_hbm.at[0], own_pair, load_sems.at[4]).start()

    peers = [
        (dr, dh, db)
        for dr in range(rows_n)
        for dh in range(heads_n)
        for db in range(cores_n)
        if (dr, dh, db) != (0, 0, 0)
    ]

    def place(offset):
        dr, dh, db = offset
        return (
            lax.rem(my_row + dr, rows_n),
            lax.rem(my_head + dh, heads_n),
            lax.rem(my_core + db, cores_n),
        )

    def target(offset):
        row, head, core = place(offset)
        return {"row": row, "head": head, "br": core}

    ordered = sorted(peers, key=lambda o: -(min(o[0], rows_n - o[0]) + o[1]))
    barrier = pltpu.get_barrier_semaphore()
    for offset in ordered:
        pl.semaphore_signal(barrier, inc=1, device_id=target(offset), device_id_type=MESH_ID)
    for load in loads[5:]:
        load.start()

    def remote(src, dst, which, offset):
        return pltpu.make_async_remote_copy(
            src_ref=src,
            dst_ref=dst,
            send_sem=send_sems.at[which],
            recv_sem=recv_sems.at[which],
            device_id=target(offset),
            device_id_type=MESH_ID,
        )

    aside = (0, 0, 1)
    other_core = lax.rem(my_core + 1, cores_n)
    near = [offset for offset in ordered if offset[2] == 0]
    for load in loads[:5]:
        load.wait()
    pl.semaphore_wait(barrier, len(peers))

    mask_f = mask_v[...].astype(jnp.float32)
    depth = mask_f.shape[1]
    pair_all[my_core, me, count : count + 1] = jnp.concatenate(
        [mask_f, jnp.zeros((1, chan - depth), jnp.float32)], axis=1
    )
    mine = pair_all.at[my_core, me, 0 : count + 1]
    for offset in near:
        remote(mine, mine, 0, offset).start()
    weight_copies = [
        remote(src, dst.at[my_core], 3 + which, aside)
        for which, (src, dst) in enumerate(
            ((tri_in_hbm, tri_in_all), (tri_bias_hbm, tri_bias_all), (tri_out_hbm, tri_out_all))
        )
    ]
    for copy in weight_copies:
        copy.start()

    pieces = seqs // 8
    aligned = align_v[:, 0, :]
    centred = aligned - jnp.mean(aligned, axis=-1, keepdims=True)
    inverse = lax.rsqrt(jnp.mean(centred * centred, axis=-1, keepdims=True) + EPSILON)
    lane = lax.broadcasted_iota(jnp.int32, (seqs, depth), 1)
    own_s = lax.broadcasted_iota(jnp.int32, (seqs, depth), 0) + my_core * seqs
    mask_own = jnp.sum(jnp.where(lane == own_s, mask_f, 0.0), axis=1, keepdims=True)
    in_hi, in_lo = split(outer_in_v[...] * gain_v[...])
    in_hi = jnp.concatenate([in_hi] * pieces, axis=0)
    in_lo = jnp.concatenate([in_lo] * pieces, axis=0)
    rows_hi, rows_lo = split(centred)

    def against(a, b):
        return lax.dot_general(a, b, (NT, ((), ())), preferred_element_type=jnp.float32)

    both = against(jnp.concatenate([rows_hi, rows_lo], axis=0), in_hi)
    projected = both[:seqs] + both[seqs:] + against(rows_hi, in_lo)
    projected = projected * (inverse * mask_own)
    piece_at = lax.broadcasted_iota(jnp.int32, (8, chan), 1) // (2 * OPC)
    packed = projected[0:8]
    for piece in range(1, pieces):
        packed = jnp.where(piece_at == piece, projected[8 * piece : 8 * piece + 8], packed)
    slot = my_core * count + me
    proj_all[slot] = packed
    for offset in ordered:
        remote(proj_all.at[slot], proj_all.at[slot], 1, offset).start()
    for load in loads[5:]:
        load.wait()

    for q in range(OPC):
        high, low = split(outer_out_v[pl.ds(q, OPC, stride=OPC), :])
        table_v[q * OPC : (q + 1) * OPC, :chan] = high
        table_v[q * OPC : (q + 1) * OPC, chan:] = low

    pairs = count * count
    lanes = head_count * pairs
    tile_row = lax.broadcasted_iota(jnp.int32, (count, count, lanes), 0)
    lane_at = lax.rem(lax.broadcasted_iota(jnp.int32, (count, count, lanes), 2), pairs)
    at_first = tile_row == lane_at // count
    at_second = tile_row == lax.rem(lane_at, count)
    live = [live_ref[n].astype(jnp.float32) for n in range(count)]
    key_at = lax.broadcasted_iota(jnp.int32, (count, lanes), 0)
    first_at = lax.broadcasted_iota(jnp.int32, (count, count, chan), 0)
    second_at = lax.broadcasted_iota(jnp.int32, (count, count, chan), 1)
    key_live = jnp.zeros((count, lanes), jnp.float32)
    live_first = jnp.zeros((count, count, chan), jnp.float32)
    live_second = jnp.zeros((count, count, chan), jnp.float32)
    for n in range(count):
        key_live = jnp.where(key_at == n, live[n], key_live)
        live_first = jnp.where(first_at == n, live[n], live_first)
        live_second = jnp.where(second_at == n, live[n], live_second)
    key_shift = (key_live - 1.0) * MASK_SHIFT
    pair_mask = (live_first * live_second).reshape(pairs, chan)
    lane_head = lax.broadcasted_iota(jnp.int32, (pairs, width), 1) // size

    def heads_apart(values):
        return jnp.concatenate(
            [jnp.where(lane_head == h, values, 0.0) for h in range(head_count)], axis=0
        )

    def spread_over(values, where):
        return jnp.where(where, values[None], 0.0).reshape(pairs, lanes)

    for copy in weight_copies:
        copy.wait_recv()

    scale = size ** (-0.5)
    for t in range(2):
        blocks = []
        for h in range(head_count):
            blocks.append(tri_in_all[h // half, t, :, h % half, :])
        bias_rows = jnp.concatenate(
            [tri_bias_all[core, t] for core in range(cores_n)]
            + [tri_gain_v[t : t + 1], jnp.zeros((chan - head_count - 1, chan), jnp.float32)],
            axis=0,
        )
        turned_rows = bias_rows.T
        gain_column = jnp.broadcast_to(turned_rows[:, head_count : head_count + 1], (chan, width))

        def keep(start, columns):
            columns = columns - jnp.mean(columns, axis=0, keepdims=True)
            high, low = split(columns)
            wide_v[t, :chan, start : start + columns.shape[1]] = high
            wide_v[t, chan:, start : start + columns.shape[1]] = low
            return columns

        kept = []
        for block in range(4):
            columns = jnp.concatenate(
                [b[:, block * size : (block + 1) * size] for b in blocks], axis=1
            )
            columns = columns * gain_column
            kept.append(keep(block * width, columns * scale if block == 0 else columns))
        bias_columns = jnp.concatenate(
            [
                jnp.broadcast_to(turned_rows[:, h : h + 1], (chan, pairs))
                for h in range(head_count)
            ],
            axis=1,
        )
        keep(4 * width, bias_columns * jnp.concatenate([gain_column] * (lanes // width), axis=1))
        weight_head = lax.broadcasted_iota(jnp.int32, (chan, width), 1) // size
        for which in range(2):
            one, other = kept[1 - which], kept[which]
            apart = jnp.concatenate(
                [jnp.where(weight_head == h, other, 0.0) for h in range(head_count)], axis=0
            )
            product = halves(plain_dot(doubled(one), stacked(apart, 1), NT))
            high, low = split(product)
            start = which * head_count * chan
            cross_v[t, :chan, start : start + head_count * chan] = high
            cross_v[t, chan:, start : start + head_count * chan] = low
        out_rows = jnp.concatenate(
            [tri_out_all[h // half, t, h % half] for h in range(head_count)], axis=0
        )
        back_v[t] = stacked(out_rows, 1)
        out_centred = out_rows - jnp.mean(out_rows, axis=1, keepdims=True)
        out_v[t] = stacked(jnp.concatenate([out_rows, out_centred], axis=1), 0)

    gathered = pair_all.at[my_core, 0 : count - 1, 0 : count + 1]
    pair_total = remote(gathered, gathered, 0, aside)
    pair_total.wait_recv()
    forward_copy = remote(
        pair_all.at[my_core, :, 0 : count + 1], pair_all.at[my_core, :, 0 : count + 1], 2, aside
    )
    forward_copy.start()
    shared = proj_all.at[0 : cores_n * count - 1]
    proj_total = remote(shared, shared, 1, aside)
    proj_total.wait_recv()

    left_tiles = []
    right_tiles = []
    for core in range(cores_n):
        for piece in range(pieces):
            base = piece * 2 * OPC
            left_tiles.append(
                jnp.concatenate(
                    [proj_all[core * count + n, :, base : base + OPC] for n in range(count)], axis=1
                )
            )
            right_tiles.append(
                jnp.concatenate(
                    [
                        proj_all[core * count + n, :, base + OPC : base + 2 * OPC]
                        for n in range(count)
                    ],
                    axis=1,
                )
            )
    left = jnp.concatenate(left_tiles, axis=0)
    right = jnp.concatenate(right_tiles, axis=0)
    mixed = pair_dot(split(right), split(left), TN)
    for block in range(mixed_v.shape[0]):
        mixed_v[block] = mixed[:, block * chan : (block + 1) * chan]
    strips = [[] for _ in range(count)]
    for q in range(OPC):
        for block in range(mixed_v.shape[0]):
            tile = mixed_v[block, pl.ds(q, count, stride=OPC), :]
            for n in range(chan // OPC):
                strips[block * (chan // OPC) + n].append(tile[:, n * OPC : (n + 1) * OPC])
    crossed = jnp.concatenate([jnp.concatenate(s, axis=1) for s in strips], axis=0)
    summed = quarters(plain_dot(stacked(crossed, 0), table_v[...], NN))
    mask_rows = jnp.concatenate(
        [pair_all[my_core, n, count : count + 1] for n in range(count)], axis=0
    )
    counts = jnp.sum(mask_rows[:, None, :] * mask_rows[None, :, :], axis=-1, keepdims=True)
    forward_copy.wait_recv()
    acts = jnp.concatenate([pair_all[0, n, 0:count] for n in range(count)], axis=0)
    pair_one = acts + summed / counts.reshape(pairs, 1)

    def turn(values):
        turn_v[...] = values
        return jnp.concatenate(
            [turn_v[pl.ds(n, count, stride=count), :] for n in range(count)], axis=0
        )

    pair_order = [h for first in range(2) for h in range(first, head_count, 2)]

    def against_pairs(rows, apart):
        half_lanes = lanes // 2
        return jnp.concatenate(
            [
                fold(halves(plain_dot(rows, apart[part * half_lanes : (part + 1) * half_lanes], NT)), part)
                for part in range(2)
            ],
            axis=1,
        )

    def fold(values, part):
        half_lanes = lanes // 2
        where = at_first[:, :, part * half_lanes : (part + 1) * half_lanes]
        return jnp.sum(jnp.where(where, values.reshape(count, count, half_lanes), 0.0), axis=0)

    def by_query(values):
        half_lanes = lanes // 2
        rows = jnp.concatenate(
            [
                jnp.where(
                    at_first[:, :, part * half_lanes : (part + 1) * half_lanes],
                    values[None, :, part * half_lanes : (part + 1) * half_lanes],
                    0.0,
                ).reshape(pairs, half_lanes)
                for part in range(2)
            ],
            axis=0,
        )

        def across(piece):
            flipped = piece.T
            return jnp.concatenate([flipped[:pairs], flipped[pairs:]], axis=1)

        return jnp.concatenate([across(piece) for piece in split(rows)], axis=0)

    def prepare_rows(centred, t):
        inverse = lax.rsqrt(jnp.mean(centred * centred, axis=-1, keepdims=True) + EPSILON)
        rows = doubled(centred)
        projected = halves(plain_dot(rows, wide_v[t], NN)) * inverse
        query, key, value, gate = (
            projected[:, block * width : (block + 1) * width] for block in range(4)
        )
        bias = jnp.sum(
            jnp.where(at_second, projected[:, 4 * width :].reshape(count, count, lanes), 0.0), axis=0
        )
        return (rows, inverse, query, key, value, jax.nn.sigmoid(gate), bias)

    def probabilities(query, key, bias):
        logits = against_pairs(doubled(key), stacked(heads_apart(query), 1)) + bias + key_shift
        top = jnp.max(logits, axis=0, keepdims=True)
        exps = jnp.exp(logits - top)
        return exps / jnp.sum(exps, axis=0, keepdims=True)

    def attend_pairs(probs, value):
        apart = jnp.concatenate(
            [jnp.where(lane_head == h, value, 0.0) for h in pair_order], axis=0
        )
        return quarters(plain_dot(by_query(probs), stacked(apart, 1), NN))

    def crossings(rows, inverse, t):
        crossed_rows = halves(plain_dot(rows, cross_v[t], NN)) * inverse

        def tall(start, order):
            return stacked(
                jnp.concatenate(
                    [crossed_rows[:, start + h * chan : start + (h + 1) * chan] for h in order], axis=0
                ),
                1,
            )

        return (tall(0, pair_order), tall(head_count * chan, range(head_count)))

    def through(probs, d_attended, gate, attended, value, key_cross, query_cross, t):
        d_mixed = stacked(heads_apart(d_attended * gate), 1)
        d_probs = against_pairs(doubled(value), d_mixed)
        d_gate = d_attended * attended * gate * (1.0 - gate)
        d_value = quarters(plain_dot(stacked(spread_over(probs, at_first), 0), d_mixed, NN))
        d_logits = probs * (d_probs - jnp.sum(probs * d_probs, axis=0, keepdims=True))
        by_key = plain_dot(stacked(spread_over(d_logits, at_first), 0), query_cross, NN)
        by_bias = plain_dot(
            stacked(spread_over(d_logits, at_second), 0), wide_v[t, :, 4 * width :], NT
        )
        by_rest = plain_dot(
            stacked(jnp.concatenate([d_value, d_gate], axis=1), 0),
            wide_v[t, :, 2 * width : 4 * width],
            NT,
        )
        by_queries = plain_dot(by_query(d_logits), key_cross, NN)
        return quarters(by_rest + by_key + by_bias + by_queries)

    centred_one = pair_one - jnp.mean(pair_one, axis=-1, keepdims=True)
    rows_0, inverse_0, query_0, key_0, value_0, gate_0, bias_0 = prepare_rows(centred_one, 0)
    probs_0 = probabilities(query_0, key_0, bias_0)
    attended_0 = attend_pairs(probs_0, value_0)
    update = halves(plain_dot(doubled(gate_0 * attended_0), out_v[0], NN))
    pair_two = pair_one + update[:, :chan] * pair_mask
    centred_two = turn(centred_one + update[:, chan:] * pair_mask)
    cot = jnp.concatenate([pair_all[1, :, n, :] for n in range(count)], axis=0)
    d_attended_1 = halves(plain_dot(doubled(cot * pair_mask), back_v[1], NT))

    rows_1, inverse_1, query_1, key_1, value_1, gate_1, bias_1 = prepare_rows(centred_two, 1)
    probs_1 = probabilities(query_1, key_1, bias_1)
    attended_1 = attend_pairs(probs_1, value_1)
    key_cross_1, query_cross_1 = crossings(rows_1, inverse_1, 1)
    d_rows_1 = through(
        probs_1, d_attended_1, gate_1, attended_1, value_1, key_cross_1, query_cross_1, 1
    )
    update = halves(plain_dot(doubled(gate_1 * attended_1), out_v[1], NN))

    def norm_back(d_rows, centred, inverse):
        share = jnp.mean(d_rows * centred, axis=-1, keepdims=True) * (inverse * inverse)
        return inverse * (d_rows - centred * share)

    grad_two = turn(cot + norm_back(d_rows_1, centred_two, inverse_1))
    d_attended_0 = halves(plain_dot(doubled(grad_two * pair_mask), back_v[0], NT))
    key_cross_0, query_cross_0 = crossings(rows_0, inverse_0, 0)
    d_rows_0 = through(
        probs_0, d_attended_0, gate_0, attended_0, value_0, key_cross_0, query_cross_0, 0
    )
    turned = turn(pair_two) + update[:, :chan] * pair_mask
    turn_v[...] = turned
    out_ref[0] = turn_v[pl.ds(me, count, stride=count), :]
    turn_v[...] = grad_two + norm_back(d_rows_0, centred_one, inverse_0)
    out_ref[1] = turn_v[pl.ds(pl.multiple_of(me * count, count), count), :]

    for copy in (pair_total, proj_total, forward_copy, *weight_copies):
        copy.wait_send()


def fused_body(shape, args):
    (
        pair_acts,
        alignment,
        align_mask,
        residue_mask,
        align_gain,
        outer_in,
        outer_out,
        tri_gain,
        tri_in,
        tri_bias,
        tri_out,
        pair_cotangent,
    ) = args
    rows_n, heads_n, cores_n = shape["row"], shape["head"], shape["br"]
    count = rows_n * heads_n
    chan = pair_acts.shape[-1]
    seqs = alignment.shape[0]
    half, size = tri_in.shape[2], tri_in.shape[3] // 4
    head_count = half * cores_n
    lanes = head_count * count * count
    wide = 4 * head_count * size + lanes
    f32, b16 = jnp.float32, jnp.bfloat16
    anywhere = pl.BlockSpec(memory_space=pl.ANY)
    here = pl.BlockSpec(memory_space=pltpu.VMEM)
    dma = pltpu.SemaphoreType.DMA
    scratch = [
        pltpu.SMEM(residue_mask.shape, jnp.int32),
        pltpu.VMEM((cores_n, count, count + 8, chan), f32),
        pltpu.VMEM((cores_n * count, 8, chan), f32),
        pltpu.VMEM(alignment.shape, f32),
        pltpu.VMEM(align_mask.shape[::-1], jnp.int32),
        pltpu.VMEM((1, align_gain.shape[0]), f32),
        pltpu.VMEM(outer_in.shape[::-1], f32),
        pltpu.VMEM(outer_out.shape, f32),
        pltpu.VMEM(tri_gain.shape, f32),
        pltpu.VMEM((cores_n,) + tri_in.shape, f32),
        pltpu.VMEM((cores_n, 2, half, chan), f32),
        pltpu.VMEM((cores_n,) + tri_out.shape, f32),
        pltpu.VMEM((outer_out.shape[0], 2 * chan), b16),
        pltpu.VMEM((2, 2 * chan, wide), b16),
        pltpu.VMEM((2, 2 * chan, 2 * head_count * chan), b16),
        pltpu.VMEM((2, 2 * chan, 2 * chan), b16),
        pltpu.VMEM((2, chan, 2 * chan), b16),
        pltpu.VMEM((count * count, chan), f32),
        pltpu.VMEM((count * OPC // chan, count * OPC, chan), f32),
        dma((11,)),
        dma((6,)),
        dma((6,)),
    ]
    both = pl.pallas_call(
        functools.partial(fused_kernel, (rows_n, heads_n, cores_n)),
        out_shape=pltpu.VMEM((2,) + pair_acts.shape[1:], f32),
        in_specs=[anywhere] * 12,
        out_specs=here,
        scratch_shapes=scratch,
        compiler_params=pltpu.CompilerParams(collective_id=0, has_side_effects=True),
    )(
        residue_mask,
        pair_acts,
        alignment,
        align_mask.T,
        align_gain[None],
        outer_in.T,
        outer_out,
        tri_gain,
        tri_in,
        jnp.swapaxes(tri_bias, 1, 2),
        tri_out,
        pair_cotangent,
    )
    return (both[0:1], both[1:2])


def dispatch(shape, *args):
    pair_acts, alignment, align_mask, tri_in = args[0], args[1], args[2], args[8]
    count = pair_acts.shape[1]
    head_count = tri_in.shape[2] * shape["br"]
    chan = pair_acts.shape[-1]
    fits = (
        pair_acts.shape[0] == 1
        and shape["br"] == 2
        and alignment.shape[1] == 1
        and count % 8 == 0
        and alignment.shape[0] // 8 * 2 * OPC == chan
        and align_mask.shape[0] <= chan
        and head_count * (tri_in.shape[3] // 4) == chan
        and head_count * count**4 * 4 <= FUSED_BYTES
        and head_count == 4
        and head_count * count * count == 2 * chan
    )
    return fused_body(shape, args) if fits else spread_body(*args)


def solution(mesh):
    in_specs = (
        P(("grp", "row", "head"), None, None),
        P(("grp", "br"), ("row", "head"), None),
        P("grp", ("row", "head")),
        P("grp"),
        P(),
        P(),
        P(),
        P(),
        P(None, None, "br", None),
        P(None, None, "br"),
        P(None, "br", None, None),
        P(("grp", "row", "head"), None, None),
    )
    out_specs = (P(("grp", "row", "head"), None, None), P(("grp", "row", "head"), None, None))
    return jax.shard_map(functools.partial(dispatch, dict(mesh.shape)), mesh=mesh, in_specs=in_specs, out_specs=out_specs, check_vma=False)
```

```python
import functools

import jax
import jax.numpy as jnp
from jax import lax
from jax.experimental import pallas as pl
from jax.experimental.pallas import tpu as pltpu
from jax.sharding import PartitionSpec as P

OPC = 32


PRECISE = lax.Precision.HIGHEST
EPSILON = 1e-05
MASK_SHIFT = 1000000000.0


def normalize(values, scales):
    average = jnp.mean(values, axis=-1, keepdims=True)
    centred = values - average
    spread = jnp.mean(centred * centred, axis=-1, keepdims=True)
    return centred * lax.rsqrt(spread + EPSILON) * scales


def core_total(values):
    return lax.psum(values, "br")


def reorient(values):
    turned = jnp.swapaxes(values, 0, 1)
    return lax.all_to_all(turned, ("row", "head"), split_axis=0, concat_axis=1, tiled=True)


def prepare(values, scales, weight_in, weight_bias):
    normed = normalize(values, scales)
    projected = jnp.einsum("ijc,chd->ijhd", normed, weight_in, precision=PRECISE)
    bias_local = jnp.einsum("jkc,ch->hjk", normed, weight_bias, precision=PRECISE)
    return (projected, bias_local)


def attend(projected, bias_full, key_shift, weight_out):
    head_size = projected.shape[-1] // 4
    queries = projected[..., :head_size]
    key_proj = projected[..., head_size : 2 * head_size]
    value_proj = projected[..., 2 * head_size : 3 * head_size]
    gating = projected[..., 3 * head_size :]
    logits = jnp.einsum("ijhd,ikhd->ihjk", queries, key_proj, precision=PRECISE) * head_size ** (
        -0.5
    )
    logits = logits + bias_full[None] + key_shift
    attention = jax.nn.softmax(logits, axis=-1)
    attended = jnp.einsum("ihjk,ikhd->ijhd", attention, value_proj, precision=PRECISE)
    gated_out = jax.nn.sigmoid(gating) * attended
    return jnp.einsum("ijhd,hdc->ijc", gated_out, weight_out, precision=PRECISE)


def tri_forward(rows_in, scales, weight_in, weight_bias, weight_out, key_shift, pair_mask):

    def local_prep(values):
        return prepare(values, scales, weight_in, weight_bias)

    (projected, bias_local), pull_prep = jax.vjp(local_prep, rows_in)
    bias_full = lax.all_gather(bias_local, ("row", "head"), axis=1, tiled=True)

    def local_attend(proj_in, bias_in):
        return attend(proj_in, bias_in, key_shift, weight_out)

    partial_out, pull_attend = jax.vjp(local_attend, projected, bias_full)
    total_out = core_total(partial_out)
    return (rows_in + total_out * pair_mask, (pull_prep, pull_attend))


def tri_backward(grad_out, saved, pair_mask):
    pull_prep, pull_attend = saved
    grad_proj, grad_bias = pull_attend(grad_out * pair_mask)
    grad_local = lax.psum_scatter(grad_bias, ("row", "head"), scatter_dimension=1, tiled=True)
    (grad_rows,) = pull_prep((grad_proj, grad_local))
    return grad_out + core_total(grad_rows)


def spread_body(
    pair_acts,
    alignment,
    align_mask,
    residue_mask,
    align_gain,
    outer_in,
    outer_out,
    tri_gain,
    tri_in,
    tri_bias,
    tri_out,
    pair_cotangent,
):
    row_count = pair_acts.shape[0]
    live = residue_mask.astype(jnp.float32)
    key_shift = (live - 1.0) * MASK_SHIFT
    row_live = lax.dynamic_slice_in_dim(
        live, lax.axis_index(("row", "head")) * row_count, row_count, 0
    )
    pair_mask = row_live[:, None, None] * live[None, :, None]
    seq_count = alignment.shape[0]
    mask_all = align_mask.astype(jnp.float32)
    mask_own = lax.dynamic_slice_in_dim(mask_all, lax.axis_index("br") * seq_count, seq_count, 0)
    normed = normalize(alignment, align_gain)
    projected = jnp.einsum("snc,ck->snk", normed, outer_in, precision=PRECISE)
    left_part = projected[..., :OPC] * mask_own[..., None]
    right_part = jnp.swapaxes(projected[..., OPC:] * mask_own[..., None], 1, 2)
    right_all, mask_cols = (
        lax.all_gather(right_part, ("row", "head"), axis=2, tiled=True),
        lax.all_gather(mask_all, ("row", "head"), axis=1, tiled=True),
    )
    counts = jnp.einsum("si,sj->ij", mask_all, mask_cols, precision=PRECISE)
    table = outer_out.reshape(OPC, OPC, outer_out.shape[-1])
    mixed_left = jnp.einsum("sip,pqc->siqc", left_part, table, precision=PRECISE)
    partial_outer = jnp.einsum("siqc,sqj->ijc", mixed_left, right_all, precision=PRECISE)
    outer_sum = core_total(partial_outer)
    pair_one = pair_acts + outer_sum / counts[..., None]
    pair_two, saved_start = tri_forward(
        pair_one, tri_gain[0], tri_in[0], tri_bias[0], tri_out[0], key_shift, pair_mask
    )
    turned_two = reorient(pair_two)
    turned_three, saved_end = tri_forward(
        turned_two, tri_gain[1], tri_in[1], tri_bias[1], tri_out[1], key_shift, pair_mask
    )
    pair_out = reorient(turned_three)
    grad_turned = reorient(pair_cotangent)
    grad_turned = tri_backward(grad_turned, saved_end, pair_mask)
    grad_two = reorient(grad_turned)
    pair_grad = tri_backward(grad_two, saved_start, pair_mask)
    return (pair_out, pair_grad)


MESH_ID = pl.DeviceIdType.MESH
FUSED_BYTES = 1 << 20
NN = ((1,), (0,))
NT = ((1,), (1,))
TN = ((0,), (0,))


def split(values):
    high = values.astype(jnp.bfloat16)
    low = (values - high.astype(jnp.float32)).astype(jnp.bfloat16)
    return (high, low)


def pair_dot(first, second, dims):
    def one(a, b):
        return lax.dot_general(a, b, (dims, ((), ())), preferred_element_type=jnp.float32)

    a = jnp.concatenate([first[0], first[1], first[0]], axis=dims[0][0])
    b = jnp.concatenate([second[0], second[0], second[1]], axis=dims[1][0])
    return one(a, b)


def plain_dot(a, b, dims):
    return lax.dot_general(a, b, (dims, ((), ())), preferred_element_type=jnp.float32)


def doubled(values):
    high, low = split(values)
    return jnp.concatenate(
        [
            jnp.concatenate([high, high], axis=1),
            jnp.concatenate([low, jnp.zeros_like(low)], axis=1),
        ],
        axis=0,
    )


def stacked(values, axis):
    return jnp.concatenate(split(values), axis=axis)


def halves(values):
    rows = values.shape[0] // 2
    return values[:rows] + values[rows:]


def quarters(values):
    rows, columns = values.shape[0] // 2, values.shape[1] // 2
    return values[:rows, :columns] + values[rows:, :columns] + values[:rows, columns:]


def fused_kernel(
    sizes,
    live_hbm,
    acts_hbm,
    align_hbm,
    mask_hbm,
    gain_hbm,
    outer_in_hbm,
    outer_out_hbm,
    tri_gain_hbm,
    tri_in_hbm,
    tri_bias_hbm,
    tri_out_hbm,
    cot_hbm,
    out_ref,
    live_ref,
    pair_all,
    proj_all,
    align_v,
    mask_v,
    gain_v,
    outer_in_v,
    outer_out_v,
    tri_gain_v,
    tri_in_all,
    tri_bias_all,
    tri_out_all,
    table_v,
    wide_v,
    wt_v,
    comp_v,
    out_v,
    back_v,
    turn_v,
    mixed_v,
    mean_v,
    own_v,
    load_sems,
    send_sems,
    recv_sems,
):
    rows_n, heads_n, cores_n = sizes
    count = rows_n * heads_n
    chan = pair_all.shape[-1]
    my_row = lax.axis_index("row")
    my_head = lax.axis_index("head")
    my_core = lax.axis_index("br")
    me = my_row * heads_n + my_head
    seqs = align_v.shape[0]
    half = tri_in_all.shape[3]
    head_count = half * cores_n
    size = tri_in_all.shape[4] // 4
    width = head_count * size

    own_pair = pair_all.at[my_core, me, 0:count]
    loads = [
        pltpu.make_async_copy(align_hbm, align_v, load_sems.at[0]),
        pltpu.make_async_copy(gain_hbm, gain_v, load_sems.at[1]),
        pltpu.make_async_copy(outer_in_hbm, outer_in_v, load_sems.at[2]),
        pltpu.make_async_copy(mask_hbm, mask_v, load_sems.at[3]),
        pltpu.make_async_copy(acts_hbm.at[0], own_pair, load_sems.at[4]),
        pltpu.make_async_copy(tri_in_hbm, tri_in_all.at[my_core], load_sems.at[5]),
        pltpu.make_async_copy(tri_bias_hbm, tri_bias_all.at[my_core], load_sems.at[6]),
        pltpu.make_async_copy(tri_out_hbm, tri_out_all.at[my_core], load_sems.at[7]),
        pltpu.make_async_copy(live_hbm, live_ref, load_sems.at[8]),
        pltpu.make_async_copy(outer_out_hbm, outer_out_v, load_sems.at[9]),
        pltpu.make_async_copy(tri_gain_hbm, tri_gain_v, load_sems.at[10]),
    ]
    for load in loads[:4]:
        load.start()

    @pl.when(my_core == 0)
    def _():
        loads[4].start()

    @pl.when(my_core != 0)
    def _():
        pltpu.make_async_copy(cot_hbm.at[0], own_pair, load_sems.at[4]).start()

    peers = [
        (dr, dh, db)
        for dr in range(rows_n)
        for dh in range(heads_n)
        for db in range(cores_n)
        if (dr, dh, db) != (0, 0, 0)
    ]

    def place(offset):
        dr, dh, db = offset
        return (
            lax.rem(my_row + dr, rows_n),
            lax.rem(my_head + dh, heads_n),
            lax.rem(my_core + db, cores_n),
        )

    def target(offset):
        row, head, core = place(offset)
        return {"row": row, "head": head, "br": core}

    ordered = sorted(peers, key=lambda o: -(min(o[0], rows_n - o[0]) + o[1]))
    barrier = pltpu.get_barrier_semaphore()
    for offset in ordered:
        pl.semaphore_signal(barrier, inc=1, device_id=target(offset), device_id_type=MESH_ID)
    for load in loads[5:]:
        load.start()

    def remote(src, dst, which, offset):
        return pltpu.make_async_remote_copy(
            src_ref=src,
            dst_ref=dst,
            send_sem=send_sems.at[which],
            recv_sem=recv_sems.at[which],
            device_id=target(offset),
            device_id_type=MESH_ID,
        )

    aside = (0, 0, 1)
    other_core = lax.rem(my_core + 1, cores_n)
    near = [offset for offset in ordered if offset[2] == 0]
    for load in loads[:8]:
        load.wait()
    pl.semaphore_wait(barrier, len(peers))

    mask_f = mask_v[...].astype(jnp.float32)
    depth = mask_f.shape[1]
    pair_all[my_core, me, count : count + 1] = jnp.concatenate(
        [mask_f, jnp.zeros((1, chan - depth), jnp.float32)], axis=1
    )
    mine = pair_all.at[my_core, me, 0 : count + 1]
    weight_copies = [
        remote(ref.at[my_core], ref.at[my_core], 3 + which, aside)
        for which, ref in enumerate((tri_in_all, tri_bias_all, tri_out_all))
    ]
    for copy in weight_copies:
        copy.start()
    for offset in near:
        remote(mine, mine, 0, offset).start()

    pieces = seqs // 8
    aligned = align_v[:, 0, :]
    centred = aligned - jnp.mean(aligned, axis=-1, keepdims=True)
    inverse = lax.rsqrt(jnp.mean(centred * centred, axis=-1, keepdims=True) + EPSILON)
    lane = lax.broadcasted_iota(jnp.int32, (seqs, depth), 1)
    own_s = lax.broadcasted_iota(jnp.int32, (seqs, depth), 0) + my_core * seqs
    mask_own = jnp.sum(jnp.where(lane == own_s, mask_f, 0.0), axis=1, keepdims=True)
    in_hi, in_lo = split(outer_in_v[...] * gain_v[...])
    in_hi = jnp.concatenate([in_hi] * pieces, axis=0)
    in_lo = jnp.concatenate([in_lo] * pieces, axis=0)
    rows_hi, rows_lo = split(centred)

    def against(a, b):
        return lax.dot_general(a, b, (NT, ((), ())), preferred_element_type=jnp.float32)

    both = against(jnp.concatenate([rows_hi, rows_lo], axis=0), in_hi)
    projected = both[:seqs] + both[seqs:] + against(rows_hi, in_lo)
    projected = projected * (inverse * mask_own)
    piece_at = lax.broadcasted_iota(jnp.int32, (8, chan), 1) // (2 * OPC)
    packed = projected[0:8]
    for piece in range(1, pieces):
        packed = jnp.where(piece_at == piece, projected[8 * piece : 8 * piece + 8], packed)
    slot = my_core * count + me
    proj_all[slot] = packed
    for offset in ordered:
        remote(proj_all.at[slot], proj_all.at[slot], 1, offset).start()
    for load in loads[8:]:
        load.wait()

    for q in range(OPC):
        rows = outer_out_v[pl.ds(q, OPC, stride=OPC), :]
        high, low = split(rows - jnp.mean(rows, axis=1, keepdims=True))
        table_v[q * OPC : (q + 1) * OPC, :chan] = high
        table_v[q * OPC : (q + 1) * OPC, chan:] = low
        mean_v[q * OPC : (q + 1) * OPC] = rows

    pairs = count * count
    lanes = head_count * pairs
    tile_row = lax.broadcasted_iota(jnp.int32, (count, count, lanes), 0)
    lane_at = lax.rem(lax.broadcasted_iota(jnp.int32, (count, count, lanes), 2), pairs)
    at_first = tile_row == lane_at // count
    at_second = tile_row == lax.rem(lane_at, count)
    live = [live_ref[n].astype(jnp.float32) for n in range(count)]
    key_at = lax.broadcasted_iota(jnp.int32, (count, lanes), 0)
    first_at = lax.broadcasted_iota(jnp.int32, (count, count, chan), 0)
    second_at = lax.broadcasted_iota(jnp.int32, (count, count, chan), 1)
    key_live = jnp.zeros((count, lanes), jnp.float32)
    live_first = jnp.zeros((count, count, chan), jnp.float32)
    live_second = jnp.zeros((count, count, chan), jnp.float32)
    for n in range(count):
        key_live = jnp.where(key_at == n, live[n], key_live)
        live_first = jnp.where(first_at == n, live[n], live_first)
        live_second = jnp.where(second_at == n, live[n], live_second)
    key_shift = (key_live - 1.0) * MASK_SHIFT
    pair_mask = (live_first * live_second).reshape(pairs, chan)
    lane_head = lax.broadcasted_iota(jnp.int32, (pairs, width), 1) // size

    def heads_apart(values):
        return jnp.concatenate(
            [jnp.where(lane_head == h, values, 0.0) for h in range(head_count)], axis=0
        )

    def spread_over(values, where):
        return jnp.where(where, values[None], 0.0).reshape(pairs, lanes)

    for copy in weight_copies:
        copy.wait_recv()

    ones = jnp.ones((16, chan), jnp.bfloat16)
    raw_hi, raw_lo = split(mean_v[...])
    table_mean = (plain_dot(ones, raw_hi, NT) + plain_dot(ones, raw_lo, NT))[:8] * (1.0 / chan)
    scale = size ** (-0.5)

    def bias_row(h, t):
        row = tri_bias_all[h // half, t, h % half : h % half + 1] * tri_gain_v[t : t + 1]
        return row - jnp.mean(row, axis=1, keepdims=True)

    for t in range(2):
        blocks = []
        for h in range(head_count):
            blocks.append(tri_in_all[h // half, t, :, h % half, :])
        bias_rows = jnp.concatenate(
            [tri_bias_all[core, t] for core in range(cores_n)]
            + [tri_gain_v[t : t + 1], jnp.zeros((chan - head_count - 1, chan), jnp.float32)],
            axis=0,
        )
        turned_rows = bias_rows.T
        gain_column = jnp.broadcast_to(turned_rows[:, head_count : head_count + 1], (chan, width))

        def keep(start, columns):
            columns = columns - jnp.mean(columns, axis=0, keepdims=True)
            high, low = split(columns)
            wide_v[t, :chan, start : start + columns.shape[1]] = high
            wide_v[t, chan:, start : start + columns.shape[1]] = low
            return columns

        kept = []
        for block in range(4):
            columns = jnp.concatenate(
                [b[:, block * size : (block + 1) * size] for b in blocks], axis=1
            )
            columns = columns * gain_column
            kept.append(keep(block * width, columns * scale if block == 0 else columns))
        bias_columns = jnp.concatenate(
            [
                jnp.broadcast_to(turned_rows[:, h : h + 1], (chan, pairs))
                for h in range(head_count)
            ],
            axis=1,
        )
        keep(4 * width, bias_columns * jnp.concatenate([gain_column] * (lanes // width), axis=1))
        flipped = jnp.concatenate([columns.T for columns in kept], axis=0)
        wt_v[t] = stacked(flipped, 1)
        if t == 1:
            for block in range(4):
                part = doubled(flipped[block * width : (block + 1) * width])
                comp_v[block * width : (block + 1) * width] = stacked(
                    halves(plain_dot(part, back_v[0], NT)), 1
                )
            rows = [bias_row(h, 1) for h in range(head_count)]
            rows = jnp.concatenate(
                rows + [jnp.zeros((8 - head_count, chan), jnp.float32)], axis=0
            )
            through_out = halves(plain_dot(doubled(rows), back_v[0], NT))
            comp_v[4 * width :] = stacked(
                jnp.concatenate(
                    [
                        jnp.broadcast_to(through_out[h : h + 1], (pairs, chan))
                        for h in range(head_count)
                    ],
                    axis=0,
                ),
                1,
            )
        out_rows = jnp.concatenate(
            [tri_out_all[h // half, t, h % half] for h in range(head_count)], axis=0
        )
        back_v[t] = stacked(out_rows, 1)
        out_centred = out_rows - jnp.mean(out_rows, axis=1, keepdims=True)
        out_v[t] = stacked(jnp.concatenate([out_rows, out_centred], axis=1), 0)

    gathered = pair_all.at[my_core, 0 : count - 1, 0 : count + 1]
    pair_total = remote(gathered, gathered, 0, aside)
    pair_total.wait_recv()
    forward_copy = remote(
        pair_all.at[my_core, :, 0 : count + 1], pair_all.at[my_core, :, 0 : count + 1], 2, aside
    )
    forward_copy.start()
    shared = proj_all.at[0 : cores_n * count - 1]
    proj_total = remote(shared, shared, 1, aside)
    proj_total.wait_recv()

    forward_copy.wait_recv()
    left_tiles = []
    right_tiles = []
    for core in range(cores_n):
        for piece in range(pieces):
            base = piece * 2 * OPC
            left_tiles.append(
                jnp.concatenate(
                    [proj_all[core * count + n, :, base : base + OPC] for n in range(count)], axis=1
                )
            )
            right_tiles.append(
                jnp.concatenate(
                    [
                        proj_all[core * count + n, :, base + OPC : base + 2 * OPC]
                        for n in range(count)
                    ],
                    axis=1,
                )
            )
    left = jnp.concatenate(left_tiles, axis=0)
    right = jnp.concatenate(right_tiles, axis=0)
    mixed = pair_dot(split(right), split(left), TN)
    for block in range(mixed_v.shape[0]):
        mixed_v[block] = mixed[:, block * chan : (block + 1) * chan]
    strips = [[] for _ in range(count)]
    for q in range(OPC):
        for block in range(mixed_v.shape[0]):
            tile = mixed_v[block, pl.ds(q, count, stride=OPC), :]
            for n in range(chan // OPC):
                strips[block * (chan // OPC) + n].append(tile[:, n * OPC : (n + 1) * OPC])
    crossed = jnp.concatenate([jnp.concatenate(s, axis=1) for s in strips], axis=0)
    summed = quarters(plain_dot(stacked(crossed, 0), table_v[...], NN))
    mask_rows = jnp.concatenate(
        [pair_all[my_core, n, count : count + 1] for n in range(count)], axis=0
    )
    counts = jnp.sum(mask_rows[:, None, :] * mask_rows[None, :, :], axis=-1, keepdims=True)
    acts = jnp.concatenate([pair_all[0, n, 0:count] for n in range(count)], axis=0)
    counts = counts.reshape(pairs, 1)
    centred_one = acts - jnp.mean(acts, axis=-1, keepdims=True) + summed / counts
    means = jnp.concatenate(
        [
            jnp.sum(crossed[count * n : count * (n + 1)] * table_mean, axis=-1, keepdims=True)
            for n in range(count)
        ],
        axis=0,
    )
    mean_one = jnp.mean(acts, axis=-1, keepdims=True) + means / counts

    def turn(values, number):
        turn_v[number] = values
        return jnp.concatenate(
            [turn_v[number, pl.ds(n, count, stride=count), :] for n in range(count)], axis=0
        )

    pair_order = [h for first in range(2) for h in range(first, head_count, 2)]

    def against_pairs(rows, apart):
        half_lanes = lanes // 2
        return jnp.concatenate(
            [
                fold(halves(plain_dot(rows, apart[part * half_lanes : (part + 1) * half_lanes], NT)), part)
                for part in range(2)
            ],
            axis=1,
        )

    def fold(values, part):
        half_lanes = lanes // 2
        where = at_first[:, :, part * half_lanes : (part + 1) * half_lanes]
        return jnp.sum(jnp.where(where, values.reshape(count, count, half_lanes), 0.0), axis=0)

    def by_query(values):
        half_lanes = lanes // 2
        rows = jnp.concatenate(
            [
                jnp.where(
                    at_first[:, :, part * half_lanes : (part + 1) * half_lanes],
                    values[None, :, part * half_lanes : (part + 1) * half_lanes],
                    0.0,
                ).reshape(pairs, half_lanes)
                for part in range(2)
            ],
            axis=0,
        )

        def across(piece):
            flipped = piece.T
            return jnp.concatenate([flipped[:pairs], flipped[pairs:]], axis=1)

        return jnp.concatenate([across(piece) for piece in split(rows)], axis=0)

    def prepare_rows(centred, t):
        inverse = lax.rsqrt(jnp.mean(centred * centred, axis=-1, keepdims=True) + EPSILON)
        raw = halves(plain_dot(doubled(centred), wide_v[t], NN))
        projected = raw * inverse
        query, key, value, gate = (
            projected[:, block * width : (block + 1) * width] for block in range(4)
        )
        bias = jnp.sum(
            jnp.where(at_second, projected[:, 4 * width :].reshape(count, count, lanes), 0.0), axis=0
        )
        return (raw, query, key, value, jax.nn.sigmoid(gate), bias)

    def probabilities(mixed_query, key, bias):
        logits = against_pairs(doubled(key), mixed_query) + bias + key_shift
        top = jnp.max(logits, axis=0, keepdims=True)
        exps = jnp.exp(logits - top)
        return exps / jnp.sum(exps, axis=0, keepdims=True)

    def pair_heads(values):
        return stacked(
            jnp.concatenate([jnp.where(lane_head == h, values, 0.0) for h in pair_order], axis=0), 1
        )

    def attend_pairs(probs, value):
        return quarters(plain_dot(by_query(probs), pair_heads(value), NN))

    def spread_rows(values, where):
        return stacked(spread_over(values, where), 0)

    def of_logits(probs, d_probs):
        return probs * (d_probs - jnp.sum(probs * d_probs, axis=0, keepdims=True))

    _, query_0, key_0, value_0, gate_0, bias_0 = prepare_rows(centred_one, 0)
    probs_0 = probabilities(stacked(heads_apart(query_0), 1), key_0, bias_0)
    cot = jnp.concatenate([pair_all[1, :, n, :] for n in range(count)], axis=0)
    d_attended_1 = halves(plain_dot(doubled(cot * pair_mask), back_v[1], NT))
    attended_0 = attend_pairs(probs_0, value_0)
    update = halves(plain_dot(doubled(gate_0 * attended_0), out_v[0], NN))
    centred_two = centred_one + update[:, chan:] * pair_mask
    pair_two = mean_one + centred_one + update[:, :chan] * pair_mask
    turned_two = turn(centred_two, 0)
    turned_whole = turn(pair_two, 4)
    cot_turned = turn(cot, 3)
    known = plain_dot(
        jnp.concatenate([doubled(cot_turned), doubled(centred_two)], axis=0), back_v[0], NT
    )

    raw_1, query_1, key_1, value_1, gate_1, bias_1 = prepare_rows(turned_two, 1)
    mixed_query_1 = stacked(heads_apart(query_1), 1)
    probs_1 = probabilities(mixed_query_1, key_1, bias_1)
    d_mixed_1 = stacked(heads_apart(d_attended_1 * gate_1), 1)
    d_probs_1 = against_pairs(doubled(value_1), d_mixed_1)
    d_value_1 = quarters(plain_dot(spread_rows(probs_1, at_first), d_mixed_1, NN))
    d_logits_1 = of_logits(probs_1, d_probs_1)
    d_key_1 = quarters(plain_dot(spread_rows(d_logits_1, at_first), mixed_query_1, NN))
    attended_1 = attend_pairs(probs_1, value_1)
    d_query_1 = quarters(plain_dot(by_query(d_logits_1), pair_heads(key_1), NN))
    d_gate_1 = d_attended_1 * attended_1 * gate_1 * (1.0 - gate_1)

    d_spread_1 = spread_over(d_logits_1, at_second)
    d_parts = [d_query_1, d_key_1, d_value_1, d_gate_1]
    d_out = plain_dot(stacked(d_spread_1, 0), comp_v[4 * width :], NN)
    d_out = d_out + plain_dot(
        stacked(jnp.concatenate([d_key_1, d_value_1], axis=1), 0), comp_v[width : 3 * width], NN
    )
    d_out = d_out + plain_dot(stacked(d_gate_1, 0), comp_v[3 * width : 4 * width], NN)
    d_out = d_out + plain_dot(stacked(d_query_1, 0), comp_v[:width], NN)
    d_out = turn(quarters(d_out), 1)
    d_all = d_parts + [d_spread_1[:, n * chan : (n + 1) * chan] for n in range(lanes // chan)]
    shares = sum(d * raw_1[:, n * chan : (n + 1) * chan] for n, d in enumerate(d_all))
    inverse_two = lax.rsqrt(jnp.mean(centred_two * centred_two, axis=-1, keepdims=True) + EPSILON)
    share_two = jnp.mean(turn(shares, 2), axis=-1, keepdims=True) * (inverse_two * inverse_two)
    d_attended_0 = pair_mask * (
        halves(known[: 2 * pairs])
        + inverse_two * (d_out - share_two * halves(known[2 * pairs :]))
    )

    update = halves(plain_dot(doubled(gate_1 * attended_1), out_v[1], NN))
    turn_v[5] = turned_whole + update[:, :chan] * pair_mask
    across = pl.ds(me, count, stride=count)
    out_ref[0] = turn_v[5, across, :]

    own_at = pl.ds(pl.multiple_of(me * count, count), count)

    def own(values, number):
        own_v[number] = values
        return own_v[number, own_at, :]

    def own_across(values, number):
        own_v[number] = values
        return own_v[number, across, :]

    def bias_back(d_values, t):
        total = 0.0
        for h in range(head_count):
            d_head = jnp.sum(jnp.where(lane_of_head == h, d_values, 0.0), axis=1, keepdims=True)
            total = total + d_head * bias_row(h, t)
        return total

    row_head = lax.broadcasted_iota(jnp.int32, (count, width), 1) // size

    def own_crossing(values, start, order):
        apart = jnp.concatenate([jnp.where(row_head == h, values, 0.0) for h in order], axis=0)
        rows = quarters(plain_dot(stacked(apart, 0), wt_v[0, start : start + width], NN))
        return stacked(
            jnp.concatenate(
                [
                    rows[n * count : (n + 1) * count]
                    for n in range(head_count)
                    for _ in range(count)
                ],
                axis=0,
            ),
            1,
        )

    own_first = lane_at[0] // count == me
    own_second = lax.rem(lane_at[0], count) == me
    lane_of_head = lax.broadcasted_iota(jnp.int32, (count, lanes), 1) // pairs
    key_cross_0 = own_crossing(own(key_0, 0), 0, pair_order)
    query_cross_0 = own_crossing(own(query_0, 1), width, range(head_count))
    own_gate, own_attended = own(gate_0, 2), own(attended_0, 3)
    own_centred = own(centred_one, 4)
    d_mixed_0 = stacked(heads_apart(d_attended_0 * gate_0), 1)
    d_probs_0 = against_pairs(doubled(value_0), d_mixed_0)
    d_value_0 = quarters(plain_dot(stacked(jnp.where(own_first, probs_0, 0.0), 0), d_mixed_0, NN))
    d_gate_0 = own(d_attended_0, 5) * own_attended * own_gate * (1.0 - own_gate)
    by_rest = plain_dot(
        stacked(jnp.concatenate([d_value_0, d_gate_0], axis=1), 0), wt_v[0, 2 * width :], NN
    )
    d_logits_0 = of_logits(probs_0, d_probs_0)
    by_key = plain_dot(stacked(jnp.where(own_first, d_logits_0, 0.0), 0), query_cross_0, NN)
    by_query_0 = quarters(plain_dot(by_query(d_logits_0), key_cross_0, NN))
    by_bias = bias_back(jnp.where(own_second, d_logits_0, 0.0), 0)
    d_rows_1 = quarters(
        plain_dot(
            stacked(
                jnp.concatenate([own_across(d, 8 + n) for n, d in enumerate(d_parts)], axis=1), 0
            ),
            wt_v[1],
            NN,
        )
    )
    own_spread = jnp.concatenate([own_across(d, 12 + n) for n, d in enumerate(d_all[4:])], axis=1)
    d_rows_1 = d_rows_1 + bias_back(own_spread, 1)
    own_two = own(centred_two, 7)
    spread_share = own(jnp.broadcast_to(share_two, (pairs, chan)), 14)
    spread_inverse = own(jnp.broadcast_to(inverse_two, (pairs, chan)), 15)
    own_grad = own(cot_turned, 16) + spread_inverse * (d_rows_1 - spread_share * own_two)
    d_rows_0 = quarters(by_rest + by_key) + by_bias + own(by_query_0, 6)
    own_inverse = lax.rsqrt(jnp.mean(own_centred * own_centred, axis=-1, keepdims=True) + EPSILON)
    share = jnp.mean(d_rows_0 * own_centred, axis=-1, keepdims=True) * (own_inverse * own_inverse)
    out_ref[1] = own_grad + own_inverse * (d_rows_0 - own_centred * share)

    for copy in (pair_total, proj_total, forward_copy, *weight_copies):
        copy.wait_send()


def fused_body(shape, args):
    (
        pair_acts,
        alignment,
        align_mask,
        residue_mask,
        align_gain,
        outer_in,
        outer_out,
        tri_gain,
        tri_in,
        tri_bias,
        tri_out,
        pair_cotangent,
    ) = args
    rows_n, heads_n, cores_n = shape["row"], shape["head"], shape["br"]
    count = rows_n * heads_n
    chan = pair_acts.shape[-1]
    seqs = alignment.shape[0]
    half, size = tri_in.shape[2], tri_in.shape[3] // 4
    head_count = half * cores_n
    lanes = head_count * count * count
    wide = 4 * head_count * size + lanes
    f32, b16 = jnp.float32, jnp.bfloat16
    anywhere = pl.BlockSpec(memory_space=pl.ANY)
    here = pl.BlockSpec(memory_space=pltpu.VMEM)
    dma = pltpu.SemaphoreType.DMA
    scratch = [
        pltpu.SMEM(residue_mask.shape, jnp.int32),
        pltpu.VMEM((2, count, count + 8, chan), f32),
        pltpu.VMEM((cores_n * count, 8, chan), f32),
        pltpu.VMEM(alignment.shape, f32),
        pltpu.VMEM(align_mask.shape[::-1], jnp.int32),
        pltpu.VMEM((1, align_gain.shape[0]), f32),
        pltpu.VMEM(outer_in.shape[::-1], f32),
        pltpu.VMEM(outer_out.shape, f32),
        pltpu.VMEM(tri_gain.shape, f32),
        pltpu.VMEM((cores_n,) + tri_in.shape, f32),
        pltpu.VMEM((cores_n, 2, half, chan), f32),
        pltpu.VMEM((cores_n,) + tri_out.shape, f32),
        pltpu.VMEM((outer_out.shape[0], 2 * chan), b16),
        pltpu.VMEM((2, 2 * chan, wide), b16),
        pltpu.VMEM((2, 4 * chan, 2 * chan), b16),
        pltpu.VMEM((4 * chan + lanes, 2 * chan), b16),
        pltpu.VMEM((2, 2 * chan, 2 * chan), b16),
        pltpu.VMEM((2, chan, 2 * chan), b16),
        pltpu.VMEM((6, count * count, chan), f32),
        pltpu.VMEM((count * OPC // chan, count * OPC, chan), f32),
        pltpu.VMEM(outer_out.shape, f32),
        pltpu.VMEM((17, count * count, chan), f32),
        dma((11,)),
        dma((6,)),
        dma((6,)),
    ]
    both = pl.pallas_call(
        functools.partial(fused_kernel, (rows_n, heads_n, cores_n)),
        out_shape=pltpu.VMEM((2,) + pair_acts.shape[1:], f32),
        in_specs=[anywhere] * 12,
        out_specs=here,
        scratch_shapes=scratch,
        compiler_params=pltpu.CompilerParams(collective_id=0, has_side_effects=True),
    )(
        residue_mask,
        pair_acts,
        alignment,
        align_mask.T,
        align_gain[None],
        outer_in.T,
        outer_out,
        tri_gain,
        tri_in,
        jnp.swapaxes(tri_bias, 1, 2),
        tri_out,
        pair_cotangent,
    )
    return (both[0:1], both[1:2])


def dispatch(shape, *args):
    pair_acts, alignment, align_mask, tri_in = args[0], args[1], args[2], args[8]
    count = pair_acts.shape[1]
    head_count = tri_in.shape[2] * shape["br"]
    chan = pair_acts.shape[-1]
    fits = (
        pair_acts.shape[0] == 1
        and shape["br"] == 2
        and alignment.shape[1] == 1
        and count % 8 == 0
        and alignment.shape[0] // 8 * 2 * OPC == chan
        and align_mask.shape[0] <= chan
        and head_count * (tri_in.shape[3] // 4) == chan
        and head_count * count**4 * 4 <= FUSED_BYTES
        and head_count == 4
        and head_count * count * count == 2 * chan
    )
    return fused_body(shape, args) if fits else spread_body(*args)


def solution(mesh):
    in_specs = (
        P(("grp", "row", "head"), None, None),
        P(("grp", "br"), ("row", "head"), None),
        P("grp", ("row", "head")),
        P("grp"),
        P(),
        P(),
        P(),
        P(),
        P(None, None, "br", None),
        P(None, None, "br"),
        P(None, "br", None, None),
        P(("grp", "row", "head"), None, None),
    )
    out_specs = (P(("grp", "row", "head"), None, None), P(("grp", "row", "head"), None, None))
    return jax.shard_map(functools.partial(dispatch, dict(mesh.shape)), mesh=mesh, in_specs=in_specs, out_specs=out_specs, check_vma=False)
```

```python
import functools

import jax
import jax.numpy as jnp
from jax import lax
from jax.experimental import pallas as pl
from jax.experimental.pallas import tpu as pltpu
from jax.sharding import PartitionSpec as P

OPC = 32


PRECISE = lax.Precision.HIGHEST
EPSILON = 1e-05
MASK_SHIFT = 1000000000.0


def normalize(values, scales):
    average = jnp.mean(values, axis=-1, keepdims=True)
    centred = values - average
    spread = jnp.mean(centred * centred, axis=-1, keepdims=True)
    return centred * lax.rsqrt(spread + EPSILON) * scales


def core_total(values):
    return lax.psum(values, "br")


def reorient(values):
    turned = jnp.swapaxes(values, 0, 1)
    return lax.all_to_all(turned, ("row", "head"), split_axis=0, concat_axis=1, tiled=True)


def prepare(values, scales, weight_in, weight_bias):
    normed = normalize(values, scales)
    projected = jnp.einsum("ijc,chd->ijhd", normed, weight_in, precision=PRECISE)
    bias_local = jnp.einsum("jkc,ch->hjk", normed, weight_bias, precision=PRECISE)
    return (projected, bias_local)


def attend(projected, bias_full, key_shift, weight_out):
    head_size = projected.shape[-1] // 4
    queries = projected[..., :head_size]
    key_proj = projected[..., head_size : 2 * head_size]
    value_proj = projected[..., 2 * head_size : 3 * head_size]
    gating = projected[..., 3 * head_size :]
    logits = jnp.einsum("ijhd,ikhd->ihjk", queries, key_proj, precision=PRECISE) * head_size ** (
        -0.5
    )
    logits = logits + bias_full[None] + key_shift
    attention = jax.nn.softmax(logits, axis=-1)
    attended = jnp.einsum("ihjk,ikhd->ijhd", attention, value_proj, precision=PRECISE)
    gated_out = jax.nn.sigmoid(gating) * attended
    return jnp.einsum("ijhd,hdc->ijc", gated_out, weight_out, precision=PRECISE)


def tri_forward(rows_in, scales, weight_in, weight_bias, weight_out, key_shift, pair_mask):

    def local_prep(values):
        return prepare(values, scales, weight_in, weight_bias)

    (projected, bias_local), pull_prep = jax.vjp(local_prep, rows_in)
    bias_full = lax.all_gather(bias_local, ("row", "head"), axis=1, tiled=True)

    def local_attend(proj_in, bias_in):
        return attend(proj_in, bias_in, key_shift, weight_out)

    partial_out, pull_attend = jax.vjp(local_attend, projected, bias_full)
    total_out = core_total(partial_out)
    return (rows_in + total_out * pair_mask, (pull_prep, pull_attend))


def tri_backward(grad_out, saved, pair_mask):
    pull_prep, pull_attend = saved
    grad_proj, grad_bias = pull_attend(grad_out * pair_mask)
    grad_local = lax.psum_scatter(grad_bias, ("row", "head"), scatter_dimension=1, tiled=True)
    (grad_rows,) = pull_prep((grad_proj, grad_local))
    return grad_out + core_total(grad_rows)


def spread_body(
    pair_acts,
    alignment,
    align_mask,
    residue_mask,
    align_gain,
    outer_in,
    outer_out,
    tri_gain,
    tri_in,
    tri_bias,
    tri_out,
    pair_cotangent,
):
    row_count = pair_acts.shape[0]
    live = residue_mask.astype(jnp.float32)
    key_shift = (live - 1.0) * MASK_SHIFT
    row_live = lax.dynamic_slice_in_dim(
        live, lax.axis_index(("row", "head")) * row_count, row_count, 0
    )
    pair_mask = row_live[:, None, None] * live[None, :, None]
    seq_count = alignment.shape[0]
    mask_all = align_mask.astype(jnp.float32)
    mask_own = lax.dynamic_slice_in_dim(mask_all, lax.axis_index("br") * seq_count, seq_count, 0)
    normed = normalize(alignment, align_gain)
    projected = jnp.einsum("snc,ck->snk", normed, outer_in, precision=PRECISE)
    left_part = projected[..., :OPC] * mask_own[..., None]
    right_part = jnp.swapaxes(projected[..., OPC:] * mask_own[..., None], 1, 2)
    right_all, mask_cols = (
        lax.all_gather(right_part, ("row", "head"), axis=2, tiled=True),
        lax.all_gather(mask_all, ("row", "head"), axis=1, tiled=True),
    )
    counts = jnp.einsum("si,sj->ij", mask_all, mask_cols, precision=PRECISE)
    table = outer_out.reshape(OPC, OPC, outer_out.shape[-1])
    mixed_left = jnp.einsum("sip,pqc->siqc", left_part, table, precision=PRECISE)
    partial_outer = jnp.einsum("siqc,sqj->ijc", mixed_left, right_all, precision=PRECISE)
    outer_sum = core_total(partial_outer)
    pair_one = pair_acts + outer_sum / counts[..., None]
    pair_two, saved_start = tri_forward(
        pair_one, tri_gain[0], tri_in[0], tri_bias[0], tri_out[0], key_shift, pair_mask
    )
    turned_two = reorient(pair_two)
    turned_three, saved_end = tri_forward(
        turned_two, tri_gain[1], tri_in[1], tri_bias[1], tri_out[1], key_shift, pair_mask
    )
    pair_out = reorient(turned_three)
    grad_turned = reorient(pair_cotangent)
    grad_turned = tri_backward(grad_turned, saved_end, pair_mask)
    grad_two = reorient(grad_turned)
    pair_grad = tri_backward(grad_two, saved_start, pair_mask)
    return (pair_out, pair_grad)


MESH_ID = pl.DeviceIdType.MESH
FUSED_BYTES = 1 << 20
NN = ((1,), (0,))
NT = ((1,), (1,))
TN = ((0,), (0,))


def split(values):
    high = values.astype(jnp.bfloat16)
    low = (values - high.astype(jnp.float32)).astype(jnp.bfloat16)
    return (high, low)


def pair_dot(first, second, dims):
    def one(a, b):
        return lax.dot_general(a, b, (dims, ((), ())), preferred_element_type=jnp.float32)

    a = jnp.concatenate([first[0], first[1], first[0]], axis=dims[0][0])
    b = jnp.concatenate([second[0], second[0], second[1]], axis=dims[1][0])
    return one(a, b)


def plain_dot(a, b, dims):
    return lax.dot_general(a, b, (dims, ((), ())), preferred_element_type=jnp.float32)


def doubled(values):
    high, low = split(values)
    return jnp.concatenate(
        [
            jnp.concatenate([high, high], axis=1),
            jnp.concatenate([low, jnp.zeros_like(low)], axis=1),
        ],
        axis=0,
    )


def stacked(values, axis):
    return jnp.concatenate(split(values), axis=axis)


def halves(values):
    rows = values.shape[0] // 2
    return values[:rows] + values[rows:]


def apart_dot(rows, other):
    half, columns = rows.shape[0] // 2, other.shape[1] // 2
    wide = plain_dot(rows[:half], other, NN)
    return wide[:, :columns] + wide[:, columns:] + plain_dot(rows[half:], other[:, :columns], NN)


def quarters(values):
    rows, columns = values.shape[0] // 2, values.shape[1] // 2
    return values[:rows, :columns] + values[rows:, :columns] + values[:rows, columns:]


def fused_kernel(
    sizes,
    live_hbm,
    acts_hbm,
    align_hbm,
    mask_hbm,
    gain_hbm,
    outer_in_hbm,
    outer_out_hbm,
    tri_gain_hbm,
    tri_in_hbm,
    tri_bias_hbm,
    tri_out_hbm,
    cot_hbm,
    out_ref,
    live_ref,
    pair_all,
    proj_all,
    align_v,
    mask_v,
    gain_v,
    outer_in_v,
    outer_out_v,
    tri_gain_v,
    tri_in_all,
    tri_bias_all,
    tri_out_all,
    table_v,
    wide_v,
    wt_v,
    comp_v,
    out_v,
    back_v,
    turn_v,
    mixed_v,
    mean_v,
    own_v,
    load_sems,
    send_sems,
    recv_sems,
):
    rows_n, heads_n, cores_n = sizes
    count = rows_n * heads_n
    chan = pair_all.shape[-1]
    my_row = lax.axis_index("row")
    my_head = lax.axis_index("head")
    my_core = lax.axis_index("br")
    me = my_row * heads_n + my_head
    seqs = align_v.shape[0]
    half = tri_in_all.shape[3]
    head_count = half * cores_n
    size = tri_in_all.shape[4] // 4
    width = head_count * size

    own_pair = pair_all.at[my_core, me, 0:count]
    loads = [
        pltpu.make_async_copy(align_hbm, align_v, load_sems.at[0]),
        pltpu.make_async_copy(gain_hbm, gain_v, load_sems.at[1]),
        pltpu.make_async_copy(outer_in_hbm, outer_in_v, load_sems.at[2]),
        pltpu.make_async_copy(mask_hbm, mask_v, load_sems.at[3]),
        pltpu.make_async_copy(acts_hbm.at[0], own_pair, load_sems.at[4]),
        pltpu.make_async_copy(tri_in_hbm, tri_in_all.at[my_core], load_sems.at[5]),
        pltpu.make_async_copy(tri_bias_hbm, tri_bias_all.at[my_core], load_sems.at[6]),
        pltpu.make_async_copy(tri_out_hbm, tri_out_all.at[my_core], load_sems.at[7]),
        pltpu.make_async_copy(live_hbm, live_ref, load_sems.at[8]),
        pltpu.make_async_copy(outer_out_hbm, outer_out_v, load_sems.at[9]),
        pltpu.make_async_copy(tri_gain_hbm, tri_gain_v, load_sems.at[10]),
    ]
    for load in loads[:4]:
        load.start()

    @pl.when(my_core == 0)
    def _():
        loads[4].start()

    @pl.when(my_core != 0)
    def _():
        pltpu.make_async_copy(cot_hbm.at[0], own_pair, load_sems.at[4]).start()

    peers = [
        (dr, dh, db)
        for dr in range(rows_n)
        for dh in range(heads_n)
        for db in range(cores_n)
        if (dr, dh, db) != (0, 0, 0)
    ]

    def place(offset):
        dr, dh, db = offset
        return (
            lax.rem(my_row + dr, rows_n),
            lax.rem(my_head + dh, heads_n),
            lax.rem(my_core + db, cores_n),
        )

    def target(offset):
        row, head, core = place(offset)
        return {"row": row, "head": head, "br": core}

    ordered = sorted(peers, key=lambda o: -(min(o[0], rows_n - o[0]) + o[1]))
    barrier = pltpu.get_barrier_semaphore()
    for offset in ordered:
        pl.semaphore_signal(barrier, inc=1, device_id=target(offset), device_id_type=MESH_ID)
    for load in loads[5:]:
        load.start()

    def remote(src, dst, which, offset):
        return pltpu.make_async_remote_copy(
            src_ref=src,
            dst_ref=dst,
            send_sem=send_sems.at[which],
            recv_sem=recv_sems.at[which],
            device_id=target(offset),
            device_id_type=MESH_ID,
        )

    aside = (0, 0, 1)
    other_core = lax.rem(my_core + 1, cores_n)
    near = [offset for offset in ordered if offset[2] == 0]
    for load in loads[:8]:
        load.wait()
    pl.semaphore_wait(barrier, len(peers))

    mask_f = mask_v[...].astype(jnp.float32)
    depth = mask_f.shape[1]
    pair_all[my_core, me, count : count + 1] = jnp.concatenate(
        [mask_f, jnp.zeros((1, chan - depth), jnp.float32)], axis=1
    )
    mine = pair_all.at[my_core, me, 0 : count + 1]
    weight_copies = [
        remote(ref.at[my_core], ref.at[my_core], 3 + which, aside)
        for which, ref in enumerate((tri_in_all, tri_bias_all, tri_out_all))
    ]
    for copy in weight_copies:
        copy.start()
    for offset in near:
        remote(mine, mine, 0, offset).start()

    pieces = seqs // 8
    aligned = align_v[:, 0, :]
    centred = aligned - jnp.mean(aligned, axis=-1, keepdims=True)
    inverse = lax.rsqrt(jnp.mean(centred * centred, axis=-1, keepdims=True) + EPSILON)
    lane = lax.broadcasted_iota(jnp.int32, (seqs, depth), 1)
    own_s = lax.broadcasted_iota(jnp.int32, (seqs, depth), 0) + my_core * seqs
    mask_own = jnp.sum(jnp.where(lane == own_s, mask_f, 0.0), axis=1, keepdims=True)
    in_hi, in_lo = split(outer_in_v[...] * gain_v[...])
    in_hi = jnp.concatenate([in_hi] * pieces, axis=0)
    in_lo = jnp.concatenate([in_lo] * pieces, axis=0)
    rows_hi, rows_lo = split(centred)

    def against(a, b):
        return lax.dot_general(a, b, (NT, ((), ())), preferred_element_type=jnp.float32)

    both = against(jnp.concatenate([rows_hi, rows_lo], axis=0), in_hi)
    projected = both[:seqs] + both[seqs:] + against(rows_hi, in_lo)
    projected = projected * (inverse * mask_own)
    piece_at = lax.broadcasted_iota(jnp.int32, (8, chan), 1) // (2 * OPC)
    packed = projected[0:8]
    for piece in range(1, pieces):
        packed = jnp.where(piece_at == piece, projected[8 * piece : 8 * piece + 8], packed)
    slot = my_core * count + me
    proj_all[slot] = packed
    for offset in ordered:
        remote(proj_all.at[slot], proj_all.at[slot], 1, offset).start()
    for load in loads[8:]:
        load.wait()

    for q in range(OPC):
        rows = outer_out_v[pl.ds(q, OPC, stride=OPC), :]
        high, low = split(rows - jnp.mean(rows, axis=1, keepdims=True))
        table_v[q * OPC : (q + 1) * OPC, :chan] = high
        table_v[q * OPC : (q + 1) * OPC, chan:] = low
        mean_v[q * OPC : (q + 1) * OPC] = rows

    pairs = count * count
    lanes = head_count * pairs
    tile_row = lax.broadcasted_iota(jnp.int32, (count, count, lanes), 0)
    lane_at = lax.rem(lax.broadcasted_iota(jnp.int32, (count, count, lanes), 2), pairs)
    at_first = tile_row == lane_at // count
    at_second = tile_row == lax.rem(lane_at, count)
    live = [live_ref[n].astype(jnp.float32) for n in range(count)]
    key_at = lax.broadcasted_iota(jnp.int32, (count, lanes), 0)
    first_at = lax.broadcasted_iota(jnp.int32, (count, count, chan), 0)
    second_at = lax.broadcasted_iota(jnp.int32, (count, count, chan), 1)
    key_live = jnp.zeros((count, lanes), jnp.float32)
    live_first = jnp.zeros((count, count, chan), jnp.float32)
    live_second = jnp.zeros((count, count, chan), jnp.float32)
    for n in range(count):
        key_live = jnp.where(key_at == n, live[n], key_live)
        live_first = jnp.where(first_at == n, live[n], live_first)
        live_second = jnp.where(second_at == n, live[n], live_second)
    key_shift = (key_live - 1.0) * MASK_SHIFT
    pair_mask = (live_first * live_second).reshape(pairs, chan)
    lane_head = lax.broadcasted_iota(jnp.int32, (pairs, width), 1) // size

    def heads_apart(values):
        return jnp.concatenate(
            [jnp.where(lane_head == h, values, 0.0) for h in range(head_count)], axis=0
        )

    def spread_over(values, where):
        return jnp.where(where, values[None], 0.0).reshape(pairs, lanes)

    for copy in weight_copies:
        copy.wait_recv()

    ones = jnp.ones((16, chan), jnp.bfloat16)
    raw_hi, raw_lo = split(mean_v[...])
    table_mean = (plain_dot(ones, raw_hi, NT) + plain_dot(ones, raw_lo, NT))[:8] * (1.0 / chan)
    scale = size ** (-0.5)

    def bias_row(h, t):
        row = tri_bias_all[h // half, t, h % half : h % half + 1] * tri_gain_v[t : t + 1]
        return row - jnp.mean(row, axis=1, keepdims=True)

    for t in range(2):
        blocks = []
        for h in range(head_count):
            blocks.append(tri_in_all[h // half, t, :, h % half, :])
        bias_rows = jnp.concatenate(
            [tri_bias_all[core, t] for core in range(cores_n)]
            + [tri_gain_v[t : t + 1], jnp.zeros((chan - head_count - 1, chan), jnp.float32)],
            axis=0,
        )
        turned_rows = bias_rows.T
        gain_column = jnp.broadcast_to(turned_rows[:, head_count : head_count + 1], (chan, width))

        def keep(start, columns):
            columns = columns - jnp.mean(columns, axis=0, keepdims=True)
            high, low = split(columns)
            wide_v[t, :chan, start : start + columns.shape[1]] = high
            wide_v[t, chan:, start : start + columns.shape[1]] = low
            return columns

        kept = []
        for block in range(4):
            columns = jnp.concatenate(
                [b[:, block * size : (block + 1) * size] for b in blocks], axis=1
            )
            columns = columns * gain_column
            kept.append(keep(block * width, columns * scale if block == 0 else columns))
        bias_columns = jnp.concatenate(
            [
                jnp.broadcast_to(turned_rows[:, h : h + 1], (chan, pairs))
                for h in range(head_count)
            ],
            axis=1,
        )
        keep(4 * width, bias_columns * jnp.concatenate([gain_column] * (lanes // width), axis=1))
        flipped = jnp.concatenate([columns.T for columns in kept], axis=0)
        wt_v[t] = stacked(flipped, 1)
        if t == 1:
            for block in range(4):
                part = doubled(flipped[block * width : (block + 1) * width])
                comp_v[block * width : (block + 1) * width] = stacked(
                    halves(plain_dot(part, back_v[0], NT)), 1
                )
            rows = [bias_row(h, 1) for h in range(head_count)]
            rows = jnp.concatenate(
                rows + [jnp.zeros((8 - head_count, chan), jnp.float32)], axis=0
            )
            through_out = halves(plain_dot(doubled(rows), back_v[0], NT))
            comp_v[4 * width :] = stacked(
                jnp.concatenate(
                    [
                        jnp.broadcast_to(through_out[h : h + 1], (pairs, chan))
                        for h in range(head_count)
                    ],
                    axis=0,
                ),
                1,
            )
        out_rows = jnp.concatenate(
            [tri_out_all[h // half, t, h % half] for h in range(head_count)], axis=0
        )
        back_v[t] = stacked(out_rows, 1)
        out_centred = out_rows - jnp.mean(out_rows, axis=1, keepdims=True)
        out_v[t] = stacked(jnp.concatenate([out_rows, out_centred], axis=1), 0)

    gathered = pair_all.at[my_core, 0 : count - 1, 0 : count + 1]
    pair_total = remote(gathered, gathered, 0, aside)
    pair_total.wait_recv()
    forward_copy = remote(
        pair_all.at[my_core, :, 0 : count + 1], pair_all.at[my_core, :, 0 : count + 1], 2, aside
    )
    forward_copy.start()
    shared = proj_all.at[0 : cores_n * count - 1]
    proj_total = remote(shared, shared, 1, aside)
    proj_total.wait_recv()

    forward_copy.wait_recv()
    left_tiles = []
    right_tiles = []
    for core in range(cores_n):
        for piece in range(pieces):
            base = piece * 2 * OPC
            left_tiles.append(
                jnp.concatenate(
                    [proj_all[core * count + n, :, base : base + OPC] for n in range(count)], axis=1
                )
            )
            right_tiles.append(
                jnp.concatenate(
                    [
                        proj_all[core * count + n, :, base + OPC : base + 2 * OPC]
                        for n in range(count)
                    ],
                    axis=1,
                )
            )
    left = jnp.concatenate(left_tiles, axis=0)
    right = jnp.concatenate(right_tiles, axis=0)
    mixed = pair_dot(split(right), split(left), TN)
    for block in range(mixed_v.shape[0]):
        mixed_v[block] = mixed[:, block * chan : (block + 1) * chan]
    strips = [[] for _ in range(count)]
    for q in range(OPC):
        for block in range(mixed_v.shape[0]):
            tile = mixed_v[block, pl.ds(q, count, stride=OPC), :]
            for n in range(chan // OPC):
                strips[block * (chan // OPC) + n].append(tile[:, n * OPC : (n + 1) * OPC])
    crossed = jnp.concatenate([jnp.concatenate(s, axis=1) for s in strips], axis=0)
    summed = quarters(plain_dot(stacked(crossed, 0), table_v[...], NN))
    mask_rows = jnp.concatenate(
        [pair_all[my_core, n, count : count + 1] for n in range(count)], axis=0
    )
    counts = jnp.sum(mask_rows[:, None, :] * mask_rows[None, :, :], axis=-1, keepdims=True)
    acts = jnp.concatenate([pair_all[0, n, 0:count] for n in range(count)], axis=0)
    counts = counts.reshape(pairs, 1)
    centred_one = acts - jnp.mean(acts, axis=-1, keepdims=True) + summed / counts
    means = jnp.concatenate(
        [
            jnp.sum(crossed[count * n : count * (n + 1)] * table_mean, axis=-1, keepdims=True)
            for n in range(count)
        ],
        axis=0,
    )
    mean_one = jnp.mean(acts, axis=-1, keepdims=True) + means / counts

    def turn(values, number):
        turn_v[number] = values
        return jnp.concatenate(
            [turn_v[number, pl.ds(n, count, stride=count), :] for n in range(count)], axis=0
        )

    pair_order = [h for first in range(2) for h in range(first, head_count, 2)]

    def pair_part(rows, apart, part):
        half_lanes = lanes // 2
        piece = apart[part * half_lanes : (part + 1) * half_lanes]
        return fold(halves(plain_dot(rows, piece, NT)), part)

    def against_pairs(rows, apart):
        return jnp.concatenate([pair_part(rows, apart, part) for part in range(2)], axis=1)

    def fold(values, part):
        half_lanes = lanes // 2
        where = at_first[:, :, part * half_lanes : (part + 1) * half_lanes]
        return jnp.sum(jnp.where(where, values.reshape(count, count, half_lanes), 0.0), axis=0)

    def by_query(values):
        half_lanes = lanes // 2
        rows = jnp.concatenate(
            [
                jnp.where(
                    at_first[:, :, part * half_lanes : (part + 1) * half_lanes],
                    values[None, :, part * half_lanes : (part + 1) * half_lanes],
                    0.0,
                ).reshape(pairs, half_lanes)
                for part in range(2)
            ],
            axis=0,
        )

        def across(piece):
            flipped = piece.T
            return jnp.concatenate([flipped[:pairs], flipped[pairs:]], axis=1)

        return jnp.concatenate([across(piece) for piece in split(rows)], axis=0)

    def prepare_rows(centred, t):
        inverse = lax.rsqrt(jnp.mean(centred * centred, axis=-1, keepdims=True) + EPSILON)
        rows = doubled(centred)
        raw_qk = halves(plain_dot(rows, wide_v[t, :, : 2 * width], NN))
        raw_bias = halves(plain_dot(rows, wide_v[t, :, 4 * width :], NN))
        raw_vg = halves(plain_dot(rows, wide_v[t, :, 2 * width : 4 * width], NN))
        raw = jnp.concatenate([raw_qk, raw_vg], axis=1)
        projected = raw * inverse
        query, key, value, gate = (
            projected[:, block * width : (block + 1) * width] for block in range(4)
        )
        bias = jnp.sum(
            jnp.where(at_second, (raw_bias * inverse).reshape(count, count, lanes), 0.0), axis=0
        )
        return ((raw, raw_bias), query, key, value, gate, bias)

    def probabilities(products, bias):
        logits = products + bias + key_shift
        top = jnp.max(logits, axis=0, keepdims=True)
        exps = jnp.exp(logits - top)
        return exps / jnp.sum(exps, axis=0, keepdims=True)

    def pair_heads(values):
        return stacked(
            jnp.concatenate([jnp.where(lane_head == h, values, 0.0) for h in pair_order], axis=0), 1
        )

    def attend_pairs(probs, value):
        return apart_dot(by_query(probs), pair_heads(value))

    def spread_rows(values, where):
        return stacked(spread_over(values, where), 0)

    def of_logits(probs, d_probs):
        return probs * (d_probs - jnp.sum(probs * d_probs, axis=0, keepdims=True))

    _, query_0, key_0, value_0, gate_in_0, bias_0 = prepare_rows(centred_one, 0)
    gate_0 = jax.nn.sigmoid(gate_in_0)
    products_0 = against_pairs(doubled(key_0), stacked(heads_apart(query_0), 1))
    probs_0 = probabilities(products_0, bias_0)
    cot = jnp.concatenate([pair_all[1, :, n, :] for n in range(count)], axis=0)
    d_attended_1 = halves(plain_dot(doubled(cot * pair_mask), back_v[1], NT))
    attended_0 = attend_pairs(probs_0, value_0)
    update = halves(plain_dot(doubled(gate_0 * attended_0), out_v[0], NN))
    centred_two = centred_one + update[:, chan:] * pair_mask
    pair_two = mean_one + centred_one + update[:, :chan] * pair_mask
    turned_two = turn(centred_two, 0)
    turned_whole = turn(pair_two, 4)
    cot_turned = turn(cot, 3)
    known = plain_dot(
        jnp.concatenate([doubled(cot_turned), doubled(centred_two)], axis=0), back_v[0], NT
    )

    raws_1, query_1, key_1, value_1, gate_1, bias_1 = prepare_rows(turned_two, 1)
    gate_1 = jax.nn.sigmoid(gate_1)
    raw_1 = jnp.concatenate(raws_1, axis=1)
    mixed_query_1 = stacked(heads_apart(query_1), 1)
    d_mixed_1 = stacked(heads_apart(d_attended_1 * gate_1), 1)
    keys_1, values_1 = doubled(key_1), doubled(value_1)
    products_1_0 = pair_part(keys_1, mixed_query_1, 0)
    products_1_1 = pair_part(keys_1, mixed_query_1, 1)
    d_probs_1_0 = pair_part(values_1, d_mixed_1, 0)
    d_probs_1_1 = pair_part(values_1, d_mixed_1, 1)
    probs_1 = probabilities(jnp.concatenate([products_1_0, products_1_1], axis=1), bias_1)
    d_probs_1 = jnp.concatenate([d_probs_1_0, d_probs_1_1], axis=1)
    d_value_1 = quarters(plain_dot(spread_rows(probs_1, at_first), d_mixed_1, NN))
    d_logits_1 = of_logits(probs_1, d_probs_1)
    d_key_1 = quarters(plain_dot(spread_rows(d_logits_1, at_first), mixed_query_1, NN))
    attended_1 = attend_pairs(probs_1, value_1)
    d_query_1 = quarters(plain_dot(by_query(d_logits_1), pair_heads(key_1), NN))
    d_gate_1 = d_attended_1 * attended_1 * gate_1 * (1.0 - gate_1)

    d_spread_1 = spread_over(d_logits_1, at_second)
    d_parts = [d_query_1, d_key_1, d_value_1, d_gate_1]
    d_out = plain_dot(stacked(d_spread_1, 0), comp_v[4 * width :], NN)
    d_out = d_out + plain_dot(
        stacked(jnp.concatenate([d_key_1, d_value_1], axis=1), 0), comp_v[width : 3 * width], NN
    )
    d_out = d_out + plain_dot(stacked(d_gate_1, 0), comp_v[3 * width : 4 * width], NN)
    d_out = d_out + plain_dot(stacked(d_query_1, 0), comp_v[:width], NN)
    d_out = turn(quarters(d_out), 1)
    d_all = d_parts + [d_spread_1[:, n * chan : (n + 1) * chan] for n in range(lanes // chan)]
    shares = sum(d * raw_1[:, n * chan : (n + 1) * chan] for n, d in enumerate(d_all))
    inverse_two = lax.rsqrt(jnp.mean(centred_two * centred_two, axis=-1, keepdims=True) + EPSILON)
    share_two = jnp.mean(turn(shares, 2), axis=-1, keepdims=True) * (inverse_two * inverse_two)
    d_attended_0 = pair_mask * (
        halves(known[: 2 * pairs])
        + inverse_two * (d_out - share_two * halves(known[2 * pairs :]))
    )

    update = halves(plain_dot(doubled(gate_1 * attended_1), out_v[1], NN))
    turn_v[5] = turned_whole + update[:, :chan] * pair_mask
    across = pl.ds(me, count, stride=count)
    out_ref[0] = turn_v[5, across, :]

    own_at = pl.ds(pl.multiple_of(me * count, count), count)

    def own(values, number):
        own_v[number] = values
        return own_v[number, own_at, :]

    def own_across(values, number):
        own_v[number] = values
        return own_v[number, across, :]

    def bias_back(d_values, t):
        total = 0.0
        for h in range(head_count):
            d_head = jnp.sum(jnp.where(lane_of_head == h, d_values, 0.0), axis=1, keepdims=True)
            total = total + d_head * bias_row(h, t)
        return total

    row_head = lax.broadcasted_iota(jnp.int32, (count, width), 1) // size

    def own_crossing(values, start, order):
        apart = jnp.concatenate([jnp.where(row_head == h, values, 0.0) for h in order], axis=0)
        rows = quarters(plain_dot(stacked(apart, 0), wt_v[0, start : start + width], NN))
        return stacked(
            jnp.concatenate(
                [
                    rows[n * count : (n + 1) * count]
                    for n in range(head_count)
                    for _ in range(count)
                ],
                axis=0,
            ),
            1,
        )

    own_first = lane_at[0] // count == me
    own_second = lax.rem(lane_at[0], count) == me
    own_query = own_first & (lax.rem(lane_at[0], count) == key_at)
    lane_of_head = lax.broadcasted_iota(jnp.int32, (count, lanes), 1) // pairs
    d_rows_1 = quarters(
        plain_dot(
            stacked(
                jnp.concatenate([own_across(d, 8 + n) for n, d in enumerate(d_parts)], axis=1), 0
            ),
            wt_v[1],
            NN,
        )
    )
    own_spread = jnp.concatenate([own_across(d, 12 + n) for n, d in enumerate(d_all[4:])], axis=1)
    key_cross_0 = own_crossing(own(key_0, 0), 0, pair_order)
    query_cross_0 = own_crossing(own(query_0, 1), width, range(head_count))
    own_gate, own_attended = own(gate_0, 2), own(attended_0, 3)
    own_centred = own(centred_one, 4)
    own_inverse = lax.rsqrt(jnp.mean(own_centred * own_centred, axis=-1, keepdims=True) + EPSILON)
    d_mixed_0 = stacked(heads_apart(d_attended_0 * gate_0), 1)
    d_probs_0 = against_pairs(doubled(value_0), d_mixed_0)
    d_value_0 = quarters(plain_dot(stacked(jnp.where(own_first, probs_0, 0.0), 0), d_mixed_0, NN))
    d_gate_0 = own(d_attended_0, 5) * own_attended * own_gate * (1.0 - own_gate)
    by_rest = plain_dot(
        stacked(jnp.concatenate([d_value_0, d_gate_0], axis=1), 0), wt_v[0, 2 * width :], NN
    )
    d_logits_0 = of_logits(probs_0, d_probs_0)
    by_key = plain_dot(stacked(jnp.where(own_first, d_logits_0, 0.0), 0), query_cross_0, NN)
    by_query_0 = quarters(plain_dot(by_query(d_logits_0), key_cross_0, NN))
    weighed = d_logits_0 * products_0
    per_query = jnp.where(own_query, jnp.sum(weighed, axis=0, keepdims=True), 0.0)
    parts = jnp.where(own_first, weighed, 0.0) + per_query
    parts = parts + jnp.where(own_second, d_logits_0 * bias_0, 0.0)
    parts = sum(parts[:, n * chan : (n + 1) * chan] for n in range(lanes // chan))
    parts = parts + d_value_0 * own(value_0, 17) + d_gate_0 * own(gate_in_0, 18)
    share = jnp.sum(parts, axis=-1, keepdims=True) * (own_inverse * (1.0 / chan))
    by_bias = bias_back(jnp.where(own_second, d_logits_0, 0.0), 0)
    d_rows_1 = d_rows_1 + bias_back(own_spread, 1)
    own_two = own(centred_two, 7)
    spread_share = own(jnp.broadcast_to(share_two, (pairs, chan)), 14)
    spread_inverse = own(jnp.broadcast_to(inverse_two, (pairs, chan)), 15)
    own_grad = own(cot_turned, 16) + spread_inverse * (d_rows_1 - spread_share * own_two)
    d_rows_0 = quarters(by_rest + by_key) + by_bias + own(by_query_0, 6)
    out_ref[1] = own_grad + own_inverse * (d_rows_0 - own_centred * share)

    for copy in (pair_total, proj_total, forward_copy, *weight_copies):
        copy.wait_send()


def fused_body(shape, args):
    (
        pair_acts,
        alignment,
        align_mask,
        residue_mask,
        align_gain,
        outer_in,
        outer_out,
        tri_gain,
        tri_in,
        tri_bias,
        tri_out,
        pair_cotangent,
    ) = args
    rows_n, heads_n, cores_n = shape["row"], shape["head"], shape["br"]
    count = rows_n * heads_n
    chan = pair_acts.shape[-1]
    seqs = alignment.shape[0]
    half, size = tri_in.shape[2], tri_in.shape[3] // 4
    head_count = half * cores_n
    lanes = head_count * count * count
    wide = 4 * head_count * size + lanes
    f32, b16 = jnp.float32, jnp.bfloat16
    anywhere = pl.BlockSpec(memory_space=pl.ANY)
    here = pl.BlockSpec(memory_space=pltpu.VMEM)
    dma = pltpu.SemaphoreType.DMA
    scratch = [
        pltpu.SMEM(residue_mask.shape, jnp.int32),
        pltpu.VMEM((2, count, count + 8, chan), f32),
        pltpu.VMEM((cores_n * count, 8, chan), f32),
        pltpu.VMEM(alignment.shape, f32),
        pltpu.VMEM(align_mask.shape[::-1], jnp.int32),
        pltpu.VMEM((1, align_gain.shape[0]), f32),
        pltpu.VMEM(outer_in.shape[::-1], f32),
        pltpu.VMEM(outer_out.shape, f32),
        pltpu.VMEM(tri_gain.shape, f32),
        pltpu.VMEM((cores_n,) + tri_in.shape, f32),
        pltpu.VMEM((cores_n, 2, half, chan), f32),
        pltpu.VMEM((cores_n,) + tri_out.shape, f32),
        pltpu.VMEM((outer_out.shape[0], 2 * chan), b16),
        pltpu.VMEM((2, 2 * chan, wide), b16),
        pltpu.VMEM((2, 4 * chan, 2 * chan), b16),
        pltpu.VMEM((4 * chan + lanes, 2 * chan), b16),
        pltpu.VMEM((2, 2 * chan, 2 * chan), b16),
        pltpu.VMEM((2, chan, 2 * chan), b16),
        pltpu.VMEM((6, count * count, chan), f32),
        pltpu.VMEM((count * OPC // chan, count * OPC, chan), f32),
        pltpu.VMEM(outer_out.shape, f32),
        pltpu.VMEM((19, count * count, chan), f32),
        dma((11,)),
        dma((6,)),
        dma((6,)),
    ]
    both = pl.pallas_call(
        functools.partial(fused_kernel, (rows_n, heads_n, cores_n)),
        out_shape=pltpu.VMEM((2,) + pair_acts.shape[1:], f32),
        in_specs=[anywhere] * 12,
        out_specs=here,
        scratch_shapes=scratch,
        compiler_params=pltpu.CompilerParams(collective_id=0, has_side_effects=True),
    )(
        residue_mask,
        pair_acts,
        alignment,
        align_mask.T,
        align_gain[None],
        outer_in.T,
        outer_out,
        tri_gain,
        tri_in,
        jnp.swapaxes(tri_bias, 1, 2),
        tri_out,
        pair_cotangent,
    )
    return (both[0:1], both[1:2])


def dispatch(shape, *args):
    pair_acts, alignment, align_mask, tri_in = args[0], args[1], args[2], args[8]
    count = pair_acts.shape[1]
    head_count = tri_in.shape[2] * shape["br"]
    chan = pair_acts.shape[-1]
    fits = (
        pair_acts.shape[0] == 1
        and shape["br"] == 2
        and alignment.shape[1] == 1
        and count % 8 == 0
        and alignment.shape[0] // 8 * 2 * OPC == chan
        and align_mask.shape[0] <= chan
        and head_count * (tri_in.shape[3] // 4) == chan
        and head_count * count**4 * 4 <= FUSED_BYTES
        and head_count == 4
        and head_count * count * count == 2 * chan
    )
    return fused_body(shape, args) if fits else spread_body(*args)


def solution(mesh):
    in_specs = (
        P(("grp", "row", "head"), None, None),
        P(("grp", "br"), ("row", "head"), None),
        P("grp", ("row", "head")),
        P("grp"),
        P(),
        P(),
        P(),
        P(),
        P(None, None, "br", None),
        P(None, None, "br"),
        P(None, "br", None, None),
        P(("grp", "row", "head"), None, None),
    )
    out_specs = (P(("grp", "row", "head"), None, None), P(("grp", "row", "head"), None, None))
    return jax.shard_map(functools.partial(dispatch, dict(mesh.shape)), mesh=mesh, in_specs=in_specs, out_specs=out_specs, check_vma=False)
```

```python
import functools

import jax
import jax.numpy as jnp
from jax import lax
from jax.experimental import pallas as pl
from jax.experimental.pallas import tpu as pltpu
from jax.sharding import PartitionSpec as P

OPC = 32


PRECISE = lax.Precision.HIGHEST
EPSILON = 1e-05
MASK_SHIFT = 1000000000.0


def normalize(values, scales):
    average = jnp.mean(values, axis=-1, keepdims=True)
    centred = values - average
    spread = jnp.mean(centred * centred, axis=-1, keepdims=True)
    return centred * lax.rsqrt(spread + EPSILON) * scales


def core_total(values):
    return lax.psum(values, "br")


def reorient(values):
    turned = jnp.swapaxes(values, 0, 1)
    return lax.all_to_all(turned, ("row", "head"), split_axis=0, concat_axis=1, tiled=True)


def prepare(values, scales, weight_in, weight_bias):
    normed = normalize(values, scales)
    projected = jnp.einsum("ijc,chd->ijhd", normed, weight_in, precision=PRECISE)
    bias_local = jnp.einsum("jkc,ch->hjk", normed, weight_bias, precision=PRECISE)
    return (projected, bias_local)


def attend(projected, bias_full, key_shift, weight_out):
    head_size = projected.shape[-1] // 4
    queries = projected[..., :head_size]
    key_proj = projected[..., head_size : 2 * head_size]
    value_proj = projected[..., 2 * head_size : 3 * head_size]
    gating = projected[..., 3 * head_size :]
    logits = jnp.einsum("ijhd,ikhd->ihjk", queries, key_proj, precision=PRECISE) * head_size ** (
        -0.5
    )
    logits = logits + bias_full[None] + key_shift
    attention = jax.nn.softmax(logits, axis=-1)
    attended = jnp.einsum("ihjk,ikhd->ijhd", attention, value_proj, precision=PRECISE)
    gated_out = jax.nn.sigmoid(gating) * attended
    return jnp.einsum("ijhd,hdc->ijc", gated_out, weight_out, precision=PRECISE)


def tri_forward(rows_in, scales, weight_in, weight_bias, weight_out, key_shift, pair_mask):

    def local_prep(values):
        return prepare(values, scales, weight_in, weight_bias)

    (projected, bias_local), pull_prep = jax.vjp(local_prep, rows_in)
    bias_full = lax.all_gather(bias_local, ("row", "head"), axis=1, tiled=True)

    def local_attend(proj_in, bias_in):
        return attend(proj_in, bias_in, key_shift, weight_out)

    partial_out, pull_attend = jax.vjp(local_attend, projected, bias_full)
    total_out = core_total(partial_out)
    return (rows_in + total_out * pair_mask, (pull_prep, pull_attend))


def tri_backward(grad_out, saved, pair_mask):
    pull_prep, pull_attend = saved
    grad_proj, grad_bias = pull_attend(grad_out * pair_mask)
    grad_local = lax.psum_scatter(grad_bias, ("row", "head"), scatter_dimension=1, tiled=True)
    (grad_rows,) = pull_prep((grad_proj, grad_local))
    return grad_out + core_total(grad_rows)


def spread_body(
    pair_acts,
    alignment,
    align_mask,
    residue_mask,
    align_gain,
    outer_in,
    outer_out,
    tri_gain,
    tri_in,
    tri_bias,
    tri_out,
    pair_cotangent,
):
    row_count = pair_acts.shape[0]
    live = residue_mask.astype(jnp.float32)
    key_shift = (live - 1.0) * MASK_SHIFT
    row_live = lax.dynamic_slice_in_dim(
        live, lax.axis_index(("row", "head")) * row_count, row_count, 0
    )
    pair_mask = row_live[:, None, None] * live[None, :, None]
    seq_count = alignment.shape[0]
    mask_all = align_mask.astype(jnp.float32)
    mask_own = lax.dynamic_slice_in_dim(mask_all, lax.axis_index("br") * seq_count, seq_count, 0)
    normed = normalize(alignment, align_gain)
    projected = jnp.einsum("snc,ck->snk", normed, outer_in, precision=PRECISE)
    left_part = projected[..., :OPC] * mask_own[..., None]
    right_part = jnp.swapaxes(projected[..., OPC:] * mask_own[..., None], 1, 2)
    right_all, mask_cols = (
        lax.all_gather(right_part, ("row", "head"), axis=2, tiled=True),
        lax.all_gather(mask_all, ("row", "head"), axis=1, tiled=True),
    )
    counts = jnp.einsum("si,sj->ij", mask_all, mask_cols, precision=PRECISE)
    table = outer_out.reshape(OPC, OPC, outer_out.shape[-1])
    mixed_left = jnp.einsum("sip,pqc->siqc", left_part, table, precision=PRECISE)
    partial_outer = jnp.einsum("siqc,sqj->ijc", mixed_left, right_all, precision=PRECISE)
    outer_sum = core_total(partial_outer)
    pair_one = pair_acts + outer_sum / counts[..., None]
    pair_two, saved_start = tri_forward(
        pair_one, tri_gain[0], tri_in[0], tri_bias[0], tri_out[0], key_shift, pair_mask
    )
    turned_two = reorient(pair_two)
    turned_three, saved_end = tri_forward(
        turned_two, tri_gain[1], tri_in[1], tri_bias[1], tri_out[1], key_shift, pair_mask
    )
    pair_out = reorient(turned_three)
    grad_turned = reorient(pair_cotangent)
    grad_turned = tri_backward(grad_turned, saved_end, pair_mask)
    grad_two = reorient(grad_turned)
    pair_grad = tri_backward(grad_two, saved_start, pair_mask)
    return (pair_out, pair_grad)


MESH_ID = pl.DeviceIdType.MESH
FUSED_BYTES = 1 << 20
NN = ((1,), (0,))
NT = ((1,), (1,))
TN = ((0,), (0,))


def split(values):
    high = values.astype(jnp.bfloat16)
    low = (values - high.astype(jnp.float32)).astype(jnp.bfloat16)
    return (high, low)


def pair_dot(first, second, dims):
    def one(a, b):
        return lax.dot_general(a, b, (dims, ((), ())), preferred_element_type=jnp.float32)

    a = jnp.concatenate([first[0], first[1], first[0]], axis=dims[0][0])
    b = jnp.concatenate([second[0], second[0], second[1]], axis=dims[1][0])
    return one(a, b)


def plain_dot(a, b, dims):
    return lax.dot_general(a, b, (dims, ((), ())), preferred_element_type=jnp.float32)


def doubled(values):
    high, low = split(values)
    return jnp.concatenate(
        [
            jnp.concatenate([high, high], axis=1),
            jnp.concatenate([low, jnp.zeros_like(low)], axis=1),
        ],
        axis=0,
    )


def stacked(values, axis):
    return jnp.concatenate(split(values), axis=axis)


def halves(values):
    rows = values.shape[0] // 2
    return values[:rows] + values[rows:]


def apart_dot(rows, other):
    half, columns = rows.shape[0] // 2, other.shape[1] // 2
    wide = plain_dot(rows[:half], other, NN)
    return wide[:, :columns] + wide[:, columns:] + plain_dot(rows[half:], other[:, :columns], NN)


def quarters(values):
    rows, columns = values.shape[0] // 2, values.shape[1] // 2
    return values[:rows, :columns] + values[rows:, :columns] + values[:rows, columns:]


def fused_kernel(
    sizes,
    live_hbm,
    acts_hbm,
    align_hbm,
    mask_hbm,
    gain_hbm,
    outer_in_hbm,
    outer_out_hbm,
    tri_gain_hbm,
    tri_in_hbm,
    tri_bias_hbm,
    tri_out_hbm,
    cot_hbm,
    out_ref,
    live_ref,
    pair_all,
    proj_all,
    align_v,
    mask_v,
    gain_v,
    outer_in_v,
    outer_out_v,
    tri_gain_v,
    tri_in_all,
    tri_bias_all,
    tri_out_all,
    table_v,
    wide_v,
    wt_v,
    comp_v,
    out_v,
    back_v,
    turn_v,
    mixed_v,
    mean_v,
    own_v,
    load_sems,
    send_sems,
    recv_sems,
):
    rows_n, heads_n, cores_n = sizes
    count = rows_n * heads_n
    chan = pair_all.shape[-1]
    my_row = lax.axis_index("row")
    my_head = lax.axis_index("head")
    my_core = lax.axis_index("br")
    me = my_row * heads_n + my_head
    seqs = align_v.shape[0]
    half = tri_in_all.shape[3]
    head_count = half * cores_n
    size = tri_in_all.shape[4] // 4
    width = head_count * size

    own_pair = pair_all.at[my_core, me, 0:count]
    loads = [
        pltpu.make_async_copy(align_hbm, align_v, load_sems.at[0]),
        pltpu.make_async_copy(gain_hbm, gain_v, load_sems.at[1]),
        pltpu.make_async_copy(outer_in_hbm, outer_in_v, load_sems.at[2]),
        pltpu.make_async_copy(mask_hbm, mask_v, load_sems.at[3]),
        pltpu.make_async_copy(acts_hbm.at[0], own_pair, load_sems.at[4]),
        pltpu.make_async_copy(tri_in_hbm, tri_in_all.at[my_core], load_sems.at[5]),
        pltpu.make_async_copy(tri_bias_hbm, tri_bias_all.at[my_core], load_sems.at[6]),
        pltpu.make_async_copy(tri_out_hbm, tri_out_all.at[my_core], load_sems.at[7]),
        pltpu.make_async_copy(live_hbm, live_ref, load_sems.at[8]),
        pltpu.make_async_copy(outer_out_hbm, outer_out_v, load_sems.at[9]),
        pltpu.make_async_copy(tri_gain_hbm, tri_gain_v, load_sems.at[10]),
    ]
    for load in loads[:4]:
        load.start()

    @pl.when(my_core == 0)
    def _():
        loads[4].start()

    @pl.when(my_core != 0)
    def _():
        pltpu.make_async_copy(cot_hbm.at[0], own_pair, load_sems.at[4]).start()

    peers = [
        (dr, dh, db)
        for dr in range(rows_n)
        for dh in range(heads_n)
        for db in range(cores_n)
        if (dr, dh, db) != (0, 0, 0)
    ]

    def place(offset):
        dr, dh, db = offset

        def wrap(position, shift, extent):
            if shift == 0:
                return position
            moved = position + shift
            return jnp.where(moved >= extent, moved - extent, moved)

        return (wrap(my_row, dr, rows_n), wrap(my_head, dh, heads_n), wrap(my_core, db, cores_n))

    def target(offset):
        row, head, core = place(offset)
        return {"row": row, "head": head, "br": core}

    ordered = sorted(peers, key=lambda o: -(min(o[0], rows_n - o[0]) + o[1]))
    barrier = pltpu.get_barrier_semaphore()
    for offset in ordered:
        pl.semaphore_signal(barrier, inc=1, device_id=target(offset), device_id_type=MESH_ID)
    for load in loads[5:]:
        load.start()

    def remote(src, dst, which, offset):
        return pltpu.make_async_remote_copy(
            src_ref=src,
            dst_ref=dst,
            send_sem=send_sems.at[which],
            recv_sem=recv_sems.at[which],
            device_id=target(offset),
            device_id_type=MESH_ID,
        )

    aside = (0, 0, 1)
    other_core = lax.rem(my_core + 1, cores_n)
    near = [offset for offset in ordered if offset[2] == 0]
    for load in loads[:8]:
        load.wait()
    pl.semaphore_wait(barrier, len(peers))

    mask_f = mask_v[...].astype(jnp.float32)
    depth = mask_f.shape[1]
    pair_all[my_core, me, count : count + 1] = jnp.concatenate(
        [mask_f, jnp.zeros((1, chan - depth), jnp.float32)], axis=1
    )
    mine = pair_all.at[my_core, me, 0 : count + 1]
    weight_copies = [
        remote(ref.at[my_core], ref.at[my_core], 3 + which, aside)
        for which, ref in enumerate((tri_in_all, tri_bias_all, tri_out_all))
    ]
    for copy in weight_copies:
        copy.start()
    for offset in near:
        remote(mine, mine, 0, offset).start()

    pieces = seqs // 8
    aligned = align_v[:, 0, :]
    centred = aligned - jnp.mean(aligned, axis=-1, keepdims=True)
    inverse = lax.rsqrt(jnp.mean(centred * centred, axis=-1, keepdims=True) + EPSILON)
    lane = lax.broadcasted_iota(jnp.int32, (seqs, depth), 1)
    own_s = lax.broadcasted_iota(jnp.int32, (seqs, depth), 0) + my_core * seqs
    mask_own = jnp.sum(jnp.where(lane == own_s, mask_f, 0.0), axis=1, keepdims=True)
    in_hi, in_lo = split(outer_in_v[...] * gain_v[...])
    in_hi = jnp.concatenate([in_hi] * pieces, axis=0)
    in_lo = jnp.concatenate([in_lo] * pieces, axis=0)
    rows_hi, rows_lo = split(centred)

    def against(a, b):
        return lax.dot_general(a, b, (NT, ((), ())), preferred_element_type=jnp.float32)

    both = against(jnp.concatenate([rows_hi, rows_lo], axis=0), in_hi)
    projected = both[:seqs] + both[seqs:] + against(rows_hi, in_lo)
    projected = projected * (inverse * mask_own)
    piece_at = lax.broadcasted_iota(jnp.int32, (8, chan), 1) // (2 * OPC)
    packed = projected[0:8]
    for piece in range(1, pieces):
        packed = jnp.where(piece_at == piece, projected[8 * piece : 8 * piece + 8], packed)
    slot = my_core * count + me
    proj_all[slot] = packed
    for offset in ordered:
        remote(proj_all.at[slot], proj_all.at[slot], 1, offset).start()
    for load in loads[8:]:
        load.wait()

    for q in range(OPC):
        rows = outer_out_v[pl.ds(q, OPC, stride=OPC), :]
        high, low = split(rows - jnp.mean(rows, axis=1, keepdims=True))
        table_v[q * OPC : (q + 1) * OPC, :chan] = high
        table_v[q * OPC : (q + 1) * OPC, chan:] = low
        mean_v[q * OPC : (q + 1) * OPC] = rows

    pairs = count * count
    lanes = head_count * pairs
    tile_row = lax.broadcasted_iota(jnp.int32, (count, count, lanes), 0)
    lane_at = lax.rem(lax.broadcasted_iota(jnp.int32, (count, count, lanes), 2), pairs)
    at_first = tile_row == lane_at // count
    at_second = tile_row == lax.rem(lane_at, count)
    live = [live_ref[n].astype(jnp.float32) for n in range(count)]
    key_at = lax.broadcasted_iota(jnp.int32, (count, lanes), 0)
    first_at = lax.broadcasted_iota(jnp.int32, (count, count, chan), 0)
    second_at = lax.broadcasted_iota(jnp.int32, (count, count, chan), 1)
    key_live = jnp.zeros((count, lanes), jnp.float32)
    live_first = jnp.zeros((count, count, chan), jnp.float32)
    live_second = jnp.zeros((count, count, chan), jnp.float32)
    for n in range(count):
        key_live = jnp.where(key_at == n, live[n], key_live)
        live_first = jnp.where(first_at == n, live[n], live_first)
        live_second = jnp.where(second_at == n, live[n], live_second)
    key_shift = (key_live - 1.0) * MASK_SHIFT
    pair_mask = (live_first * live_second).reshape(pairs, chan)
    lane_head = lax.broadcasted_iota(jnp.int32, (pairs, width), 1) // size

    def heads_apart(values):
        return jnp.concatenate(
            [jnp.where(lane_head == h, values, 0.0) for h in range(head_count)], axis=0
        )

    def spread_over(values, where):
        return jnp.where(where, values[None], 0.0).reshape(pairs, lanes)

    for copy in weight_copies:
        copy.wait_recv()

    ones = jnp.ones((16, chan), jnp.bfloat16)
    raw_hi, raw_lo = split(mean_v[...])
    table_mean = (plain_dot(ones, raw_hi, NT) + plain_dot(ones, raw_lo, NT))[:8] * (1.0 / chan)
    scale = size ** (-0.5)

    def bias_row(h, t):
        row = tri_bias_all[h // half, t, h % half : h % half + 1] * tri_gain_v[t : t + 1]
        return row - jnp.mean(row, axis=1, keepdims=True)

    for t in range(2):
        blocks = []
        for h in range(head_count):
            blocks.append(tri_in_all[h // half, t, :, h % half, :])
        bias_rows = jnp.concatenate(
            [tri_bias_all[core, t] for core in range(cores_n)]
            + [tri_gain_v[t : t + 1], jnp.zeros((chan - head_count - 1, chan), jnp.float32)],
            axis=0,
        )
        turned_rows = bias_rows.T
        gain_column = jnp.broadcast_to(turned_rows[:, head_count : head_count + 1], (chan, width))

        def keep(start, columns):
            columns = columns - jnp.mean(columns, axis=0, keepdims=True)
            high, low = split(columns)
            wide_v[t, :chan, start : start + columns.shape[1]] = high
            wide_v[t, chan:, start : start + columns.shape[1]] = low
            return columns

        kept = []
        for block in range(4):
            columns = jnp.concatenate(
                [b[:, block * size : (block + 1) * size] for b in blocks], axis=1
            )
            columns = columns * gain_column
            kept.append(keep(block * width, columns * scale if block == 0 else columns))
        bias_columns = jnp.concatenate(
            [
                jnp.broadcast_to(turned_rows[:, h : h + 1], (chan, pairs))
                for h in range(head_count)
            ],
            axis=1,
        )
        keep(4 * width, bias_columns * jnp.concatenate([gain_column] * (lanes // width), axis=1))
        flipped = jnp.concatenate([columns.T for columns in kept], axis=0)
        wt_v[t] = stacked(flipped, 1)
        if t == 1:
            for block in range(4):
                part = doubled(flipped[block * width : (block + 1) * width])
                comp_v[block * width : (block + 1) * width] = stacked(
                    halves(plain_dot(part, back_v[0], NT)), 1
                )
            rows = [bias_row(h, 1) for h in range(head_count)]
            rows = jnp.concatenate(
                rows + [jnp.zeros((8 - head_count, chan), jnp.float32)], axis=0
            )
            through_out = halves(plain_dot(doubled(rows), back_v[0], NT))
            comp_v[4 * width :] = stacked(
                jnp.concatenate(
                    [
                        jnp.broadcast_to(through_out[h : h + 1], (pairs, chan))
                        for h in range(head_count)
                    ],
                    axis=0,
                ),
                1,
            )
        out_rows = jnp.concatenate(
            [tri_out_all[h // half, t, h % half] for h in range(head_count)], axis=0
        )
        back_v[t] = stacked(out_rows, 1)
        out_centred = out_rows - jnp.mean(out_rows, axis=1, keepdims=True)
        out_v[t] = stacked(jnp.concatenate([out_rows, out_centred], axis=1), 0)

    gathered = pair_all.at[my_core, 0 : count - 1, 0 : count + 1]
    pair_total = remote(gathered, gathered, 0, aside)
    pair_total.wait_recv()
    forward_copy = remote(
        pair_all.at[my_core, :, 0 : count + 1], pair_all.at[my_core, :, 0 : count + 1], 2, aside
    )
    forward_copy.start()
    shared = proj_all.at[0 : cores_n * count - 1]
    proj_total = remote(shared, shared, 1, aside)
    proj_total.wait_recv()

    forward_copy.wait_recv()
    left_tiles = []
    right_tiles = []
    for core in range(cores_n):
        for piece in range(pieces):
            base = piece * 2 * OPC
            left_tiles.append(
                jnp.concatenate(
                    [proj_all[core * count + n, :, base : base + OPC] for n in range(count)], axis=1
                )
            )
            right_tiles.append(
                jnp.concatenate(
                    [
                        proj_all[core * count + n, :, base + OPC : base + 2 * OPC]
                        for n in range(count)
                    ],
                    axis=1,
                )
            )
    left = jnp.concatenate(left_tiles, axis=0)
    right = jnp.concatenate(right_tiles, axis=0)
    mixed = pair_dot(split(right), split(left), TN)
    for block in range(mixed_v.shape[0]):
        mixed_v[block] = mixed[:, block * chan : (block + 1) * chan]
    strips = [[] for _ in range(count)]
    for q in range(OPC):
        for block in range(mixed_v.shape[0]):
            tile = mixed_v[block, pl.ds(q, count, stride=OPC), :]
            for n in range(chan // OPC):
                strips[block * (chan // OPC) + n].append(tile[:, n * OPC : (n + 1) * OPC])
    crossed = jnp.concatenate([jnp.concatenate(s, axis=1) for s in strips], axis=0)
    summed = quarters(plain_dot(stacked(crossed, 0), table_v[...], NN))
    mask_rows = jnp.concatenate(
        [pair_all[my_core, n, count : count + 1] for n in range(count)], axis=0
    )
    counts = jnp.sum(mask_rows[:, None, :] * mask_rows[None, :, :], axis=-1, keepdims=True)
    acts = jnp.concatenate([pair_all[0, n, 0:count] for n in range(count)], axis=0)
    counts = counts.reshape(pairs, 1)
    centred_one = acts - jnp.mean(acts, axis=-1, keepdims=True) + summed / counts
    means = jnp.concatenate(
        [
            jnp.sum(crossed[count * n : count * (n + 1)] * table_mean, axis=-1, keepdims=True)
            for n in range(count)
        ],
        axis=0,
    )
    mean_one = jnp.mean(acts, axis=-1, keepdims=True) + means / counts

    def turn(values, number):
        turn_v[number] = values
        return jnp.concatenate(
            [turn_v[number, pl.ds(n, count, stride=count), :] for n in range(count)], axis=0
        )

    pair_order = [h for first in range(2) for h in range(first, head_count, 2)]

    def pair_part(rows, apart, part):
        half_lanes = lanes // 2
        piece = apart[part * half_lanes : (part + 1) * half_lanes]
        return fold(halves(plain_dot(rows, piece, NT)), part)

    def against_pairs(rows, apart):
        return jnp.concatenate([pair_part(rows, apart, part) for part in range(2)], axis=1)

    def fold(values, part):
        half_lanes = lanes // 2
        where = at_first[:, :, part * half_lanes : (part + 1) * half_lanes]
        return jnp.sum(jnp.where(where, values.reshape(count, count, half_lanes), 0.0), axis=0)

    def by_query(values):
        half_lanes = lanes // 2
        rows = jnp.concatenate(
            [
                jnp.where(
                    at_first[:, :, part * half_lanes : (part + 1) * half_lanes],
                    values[None, :, part * half_lanes : (part + 1) * half_lanes],
                    0.0,
                ).reshape(pairs, half_lanes)
                for part in range(2)
            ],
            axis=0,
        )

        def across(piece):
            flipped = piece.T
            return jnp.concatenate([flipped[:pairs], flipped[pairs:]], axis=1)

        return jnp.concatenate([across(piece) for piece in split(rows)], axis=0)

    def prepare_rows(centred, t):
        inverse = lax.rsqrt(jnp.mean(centred * centred, axis=-1, keepdims=True) + EPSILON)
        rows = doubled(centred)
        raw_qk = halves(plain_dot(rows, wide_v[t, :, : 2 * width], NN))
        raw_bias = halves(plain_dot(rows, wide_v[t, :, 4 * width :], NN))
        raw_vg = halves(plain_dot(rows, wide_v[t, :, 2 * width : 4 * width], NN))
        raw = jnp.concatenate([raw_qk, raw_vg], axis=1)
        projected = raw * inverse
        query, key, value, gate = (
            projected[:, block * width : (block + 1) * width] for block in range(4)
        )
        bias = jnp.sum(
            jnp.where(at_second, (raw_bias * inverse).reshape(count, count, lanes), 0.0), axis=0
        )
        return ((raw, raw_bias), query, key, value, gate, bias)

    def probabilities(products, bias):
        logits = products + bias + key_shift
        top = jnp.max(logits, axis=0, keepdims=True)
        exps = jnp.exp(logits - top)
        return exps / jnp.sum(exps, axis=0, keepdims=True)

    def pair_heads(values):
        return stacked(
            jnp.concatenate([jnp.where(lane_head == h, values, 0.0) for h in pair_order], axis=0), 1
        )

    def attend_pairs(probs, value):
        return apart_dot(by_query(probs), pair_heads(value))

    def spread_rows(values, where):
        return stacked(spread_over(values, where), 0)

    def of_logits(probs, d_probs):
        return probs * (d_probs - jnp.sum(probs * d_probs, axis=0, keepdims=True))

    _, query_0, key_0, value_0, gate_in_0, bias_0 = prepare_rows(centred_one, 0)
    gate_0 = jax.nn.sigmoid(gate_in_0)
    products_0 = against_pairs(doubled(key_0), stacked(heads_apart(query_0), 1))
    probs_0 = probabilities(products_0, bias_0)
    cot = jnp.concatenate([pair_all[1, :, n, :] for n in range(count)], axis=0)
    d_attended_1 = halves(plain_dot(doubled(cot * pair_mask), back_v[1], NT))
    attended_0 = attend_pairs(probs_0, value_0)
    update = halves(plain_dot(doubled(gate_0 * attended_0), out_v[0], NN))
    centred_two = centred_one + update[:, chan:] * pair_mask
    pair_two = mean_one + centred_one + update[:, :chan] * pair_mask
    turned_two = turn(centred_two, 0)
    turned_whole = turn(pair_two, 4)
    cot_turned = turn(cot, 3)
    known = plain_dot(
        jnp.concatenate([doubled(cot_turned), doubled(centred_two)], axis=0), back_v[0], NT
    )

    raws_1, query_1, key_1, value_1, gate_1, bias_1 = prepare_rows(turned_two, 1)
    gate_1 = jax.nn.sigmoid(gate_1)
    raw_1 = jnp.concatenate(raws_1, axis=1)
    mixed_query_1 = stacked(heads_apart(query_1), 1)
    d_mixed_1 = stacked(heads_apart(d_attended_1 * gate_1), 1)
    keys_1, values_1 = doubled(key_1), doubled(value_1)
    products_1_0 = pair_part(keys_1, mixed_query_1, 0)
    products_1_1 = pair_part(keys_1, mixed_query_1, 1)
    d_probs_1_0 = pair_part(values_1, d_mixed_1, 0)
    d_probs_1_1 = pair_part(values_1, d_mixed_1, 1)
    probs_1 = probabilities(jnp.concatenate([products_1_0, products_1_1], axis=1), bias_1)
    d_probs_1 = jnp.concatenate([d_probs_1_0, d_probs_1_1], axis=1)
    d_value_1 = quarters(plain_dot(spread_rows(probs_1, at_first), d_mixed_1, NN))
    d_logits_1 = of_logits(probs_1, d_probs_1)
    d_key_1 = quarters(plain_dot(spread_rows(d_logits_1, at_first), mixed_query_1, NN))
    attended_1 = attend_pairs(probs_1, value_1)
    d_query_1 = quarters(plain_dot(by_query(d_logits_1), pair_heads(key_1), NN))
    d_gate_1 = d_attended_1 * attended_1 * gate_1 * (1.0 - gate_1)

    d_spread_1 = spread_over(d_logits_1, at_second)
    d_parts = [d_query_1, d_key_1, d_value_1, d_gate_1]
    d_out = plain_dot(stacked(d_spread_1, 0), comp_v[4 * width :], NN)
    d_out = d_out + plain_dot(
        stacked(jnp.concatenate([d_key_1, d_value_1], axis=1), 0), comp_v[width : 3 * width], NN
    )
    d_out = d_out + plain_dot(stacked(d_gate_1, 0), comp_v[3 * width : 4 * width], NN)
    d_out = d_out + plain_dot(stacked(d_query_1, 0), comp_v[:width], NN)
    d_out = turn(quarters(d_out), 1)
    d_all = d_parts + [d_spread_1[:, n * chan : (n + 1) * chan] for n in range(lanes // chan)]
    shares = sum(d * raw_1[:, n * chan : (n + 1) * chan] for n, d in enumerate(d_all))
    inverse_two = lax.rsqrt(jnp.mean(centred_two * centred_two, axis=-1, keepdims=True) + EPSILON)
    share_two = jnp.mean(turn(shares, 2), axis=-1, keepdims=True) * (inverse_two * inverse_two)
    d_attended_0 = pair_mask * (
        halves(known[: 2 * pairs])
        + inverse_two * (d_out - share_two * halves(known[2 * pairs :]))
    )

    update = halves(plain_dot(doubled(gate_1 * attended_1), out_v[1], NN))
    turn_v[5] = turned_whole + update[:, :chan] * pair_mask
    across = pl.ds(me, count, stride=count)
    out_ref[0] = turn_v[5, across, :]

    own_at = pl.ds(pl.multiple_of(me * count, count), count)

    def own(values, number):
        own_v[number] = values
        return own_v[number, own_at, :]

    def own_across(values, number):
        own_v[number] = values
        return own_v[number, across, :]

    def bias_back(d_values, t):
        total = 0.0
        for h in range(head_count):
            d_head = jnp.sum(jnp.where(lane_of_head == h, d_values, 0.0), axis=1, keepdims=True)
            total = total + d_head * bias_row(h, t)
        return total

    row_head = lax.broadcasted_iota(jnp.int32, (count, width), 1) // size

    def own_crossing(values, start, order):
        apart = jnp.concatenate([jnp.where(row_head == h, values, 0.0) for h in order], axis=0)
        rows = quarters(plain_dot(stacked(apart, 0), wt_v[0, start : start + width], NN))
        return stacked(
            jnp.concatenate(
                [
                    rows[n * count : (n + 1) * count]
                    for n in range(head_count)
                    for _ in range(count)
                ],
                axis=0,
            ),
            1,
        )

    own_first = lane_at[0] // count == me
    own_second = lax.rem(lane_at[0], count) == me
    own_query = own_first & (lax.rem(lane_at[0], count) == key_at)
    lane_of_head = lax.broadcasted_iota(jnp.int32, (count, lanes), 1) // pairs
    d_rows_1 = quarters(
        plain_dot(
            stacked(
                jnp.concatenate([own_across(d, 8 + n) for n, d in enumerate(d_parts)], axis=1), 0
            ),
            wt_v[1],
            NN,
        )
    )
    own_spread = jnp.concatenate([own_across(d, 12 + n) for n, d in enumerate(d_all[4:])], axis=1)
    key_cross_0 = own_crossing(own(key_0, 0), 0, pair_order)
    query_cross_0 = own_crossing(own(query_0, 1), width, range(head_count))
    own_gate, own_attended = own(gate_0, 2), own(attended_0, 3)
    own_centred = own(centred_one, 4)
    own_inverse = lax.rsqrt(jnp.mean(own_centred * own_centred, axis=-1, keepdims=True) + EPSILON)
    d_mixed_0 = stacked(heads_apart(d_attended_0 * gate_0), 1)
    d_probs_0 = against_pairs(doubled(value_0), d_mixed_0)
    d_value_0 = quarters(plain_dot(stacked(jnp.where(own_first, probs_0, 0.0), 0), d_mixed_0, NN))
    d_gate_0 = own(d_attended_0, 5) * own_attended * own_gate * (1.0 - own_gate)
    by_rest = plain_dot(
        stacked(jnp.concatenate([d_value_0, d_gate_0], axis=1), 0), wt_v[0, 2 * width :], NN
    )
    d_logits_0 = of_logits(probs_0, d_probs_0)
    by_key = plain_dot(stacked(jnp.where(own_first, d_logits_0, 0.0), 0), query_cross_0, NN)
    by_query_0 = quarters(plain_dot(by_query(d_logits_0), key_cross_0, NN))
    weighed = d_logits_0 * products_0
    per_query = jnp.where(own_query, jnp.sum(weighed, axis=0, keepdims=True), 0.0)
    parts = jnp.where(own_first, weighed, 0.0) + per_query
    parts = parts + jnp.where(own_second, d_logits_0 * bias_0, 0.0)
    parts = sum(parts[:, n * chan : (n + 1) * chan] for n in range(lanes // chan))
    parts = parts + d_value_0 * own(value_0, 17) + d_gate_0 * own(gate_in_0, 18)
    share = jnp.sum(parts, axis=-1, keepdims=True) * (own_inverse * (1.0 / chan))
    by_bias = bias_back(jnp.where(own_second, d_logits_0, 0.0), 0)
    d_rows_1 = d_rows_1 + bias_back(own_spread, 1)
    own_two = own(centred_two, 7)
    spread_share = own(jnp.broadcast_to(share_two, (pairs, chan)), 14)
    spread_inverse = own(jnp.broadcast_to(inverse_two, (pairs, chan)), 15)
    own_grad = own(cot_turned, 16) + spread_inverse * (d_rows_1 - spread_share * own_two)
    d_rows_0 = quarters(by_rest + by_key) + by_bias + own(by_query_0, 6)
    out_ref[1] = own_grad + own_inverse * (d_rows_0 - own_centred * share)

    for copy in (pair_total, proj_total, forward_copy, *weight_copies):
        copy.wait_send()


def fused_body(shape, args):
    (
        pair_acts,
        alignment,
        align_mask,
        residue_mask,
        align_gain,
        outer_in,
        outer_out,
        tri_gain,
        tri_in,
        tri_bias,
        tri_out,
        pair_cotangent,
    ) = args
    rows_n, heads_n, cores_n = shape["row"], shape["head"], shape["br"]
    count = rows_n * heads_n
    chan = pair_acts.shape[-1]
    seqs = alignment.shape[0]
    half, size = tri_in.shape[2], tri_in.shape[3] // 4
    head_count = half * cores_n
    lanes = head_count * count * count
    wide = 4 * head_count * size + lanes
    f32, b16 = jnp.float32, jnp.bfloat16
    anywhere = pl.BlockSpec(memory_space=pl.ANY)
    here = pl.BlockSpec(memory_space=pltpu.VMEM)
    dma = pltpu.SemaphoreType.DMA
    scratch = [
        pltpu.SMEM(residue_mask.shape, jnp.int32),
        pltpu.VMEM((2, count, count + 8, chan), f32),
        pltpu.VMEM((cores_n * count, 8, chan), f32),
        pltpu.VMEM(alignment.shape, f32),
        pltpu.VMEM(align_mask.shape[::-1], jnp.int32),
        pltpu.VMEM((1, align_gain.shape[0]), f32),
        pltpu.VMEM(outer_in.shape[::-1], f32),
        pltpu.VMEM(outer_out.shape, f32),
        pltpu.VMEM(tri_gain.shape, f32),
        pltpu.VMEM((cores_n,) + tri_in.shape, f32),
        pltpu.VMEM((cores_n, 2, half, chan), f32),
        pltpu.VMEM((cores_n,) + tri_out.shape, f32),
        pltpu.VMEM((outer_out.shape[0], 2 * chan), b16),
        pltpu.VMEM((2, 2 * chan, wide), b16),
        pltpu.VMEM((2, 4 * chan, 2 * chan), b16),
        pltpu.VMEM((4 * chan + lanes, 2 * chan), b16),
        pltpu.VMEM((2, 2 * chan, 2 * chan), b16),
        pltpu.VMEM((2, chan, 2 * chan), b16),
        pltpu.VMEM((6, count * count, chan), f32),
        pltpu.VMEM((count * OPC // chan, count * OPC, chan), f32),
        pltpu.VMEM(outer_out.shape, f32),
        pltpu.VMEM((19, count * count, chan), f32),
        dma((11,)),
        dma((6,)),
        dma((6,)),
    ]
    both = pl.pallas_call(
        functools.partial(fused_kernel, (rows_n, heads_n, cores_n)),
        out_shape=pltpu.VMEM((2,) + pair_acts.shape[1:], f32),
        in_specs=[anywhere] * 12,
        out_specs=here,
        scratch_shapes=scratch,
        compiler_params=pltpu.CompilerParams(collective_id=0, has_side_effects=True),
    )(
        residue_mask,
        pair_acts,
        alignment,
        align_mask.T,
        align_gain[None],
        outer_in.T,
        outer_out,
        tri_gain,
        tri_in,
        jnp.swapaxes(tri_bias, 1, 2),
        tri_out,
        pair_cotangent,
    )
    return (both[0:1], both[1:2])


def dispatch(shape, *args):
    pair_acts, alignment, align_mask, tri_in = args[0], args[1], args[2], args[8]
    count = pair_acts.shape[1]
    head_count = tri_in.shape[2] * shape["br"]
    chan = pair_acts.shape[-1]
    fits = (
        pair_acts.shape[0] == 1
        and shape["br"] == 2
        and alignment.shape[1] == 1
        and count % 8 == 0
        and alignment.shape[0] // 8 * 2 * OPC == chan
        and align_mask.shape[0] <= chan
        and head_count * (tri_in.shape[3] // 4) == chan
        and head_count * count**4 * 4 <= FUSED_BYTES
        and head_count == 4
        and head_count * count * count == 2 * chan
    )
    return fused_body(shape, args) if fits else spread_body(*args)


def solution(mesh):
    in_specs = (
        P(("grp", "row", "head"), None, None),
        P(("grp", "br"), ("row", "head"), None),
        P("grp", ("row", "head")),
        P("grp"),
        P(),
        P(),
        P(),
        P(),
        P(None, None, "br", None),
        P(None, None, "br"),
        P(None, "br", None, None),
        P(("grp", "row", "head"), None, None),
    )
    out_specs = (P(("grp", "row", "head"), None, None), P(("grp", "row", "head"), None, None))
    return jax.shard_map(functools.partial(dispatch, dict(mesh.shape)), mesh=mesh, in_specs=in_specs, out_specs=out_specs, check_vma=False)
```
